32 devices in a mesh: groups: 2 (over x), segment: 4 (over z), head: 4 (over y, core).
Axes of the slice: x: 2, y: 2, z: 4, core: 2. Of those that a mesh axis runs over, the one named last changes fastest.
Arguments:
- hidden_in: bfloat16 [2048, 3072], P(('groups', 'segment'), 'head'), parts along dimension 0, may hold values from -6 to 6
- latent_in: bfloat16 [2048, 3072], P(('groups', 'segment'), 'head'), parts along dimension 0, may hold values from -6 to 6
- key_values: bfloat16 [8, 2, 1024, 3072], P(('groups', 'segment'), None, None, 'head'), parts along dimension 0, may hold values from -162 to 162
- qkv_weight: bfloat16 [4, 3072, 3, 3072], P('segment', None, None, 'head'), may hold values from -0.109375 to 0.109375
- out_weight: bfloat16 [4, 3072, 3072], P('segment', 'head'), may hold values from -0.109375 to 0.109375
- modulation: float32 [4, 16, 3, 3072], P('segment'), may hold values from -1.5 to 1.5
- step_sizes: float32 [16], replicated, may hold values from 0.25 to 2
- patch_order: int32 [8], P('groups'), parts along dimension 0, may hold values from 0 to 3, each once
- tick_patch: int32 [8, 4], P('groups'), parts along dimension 0, may hold values from 0 to 3
- step_ids: int32 [8, 4], P('groups'), parts along dimension 0, may hold values from 0 to 15
Outputs:
- out_hidden: bfloat16 [2048, 3072], P(('groups', 'segment'), 'head'), parts along dimension 0
- out_latent: bfloat16 [2048, 3072], P(('groups', 'segment'), 'head'), parts along dimension 0
The draws below stay inside these ranges and needn't reach their ends.
There are 2 independent parts, one for each index of `groups`. The reference program is written for one: setup_inputs(seed, part) draws one part's arguments, and reference() takes and returns one part's arrays. A program takes and returns all parts, laid end to end along the dimension named above; an argument that names none is the same for every part. Nothing has to cross between parts.
All inputs are finite; a program needn't handle non-finite values.
Results may differ from the reference program's by a relative error of at most 0.028.
Values may be sent and summed in bfloat16 or wider, within the bound.
No kernel may reach another device: no remote copies, remote signals or barrier semaphores. Data moves between devices by JAX's collectives and lax.ppermute only.
A program may use at most 128 MiB of HBM per device.

```python
import math
import jax
import jax.numpy as jnp
from jax import lax

D = 3072
HEADS = 48
HEAD_DIM = 64
PATCH = 256
NPATCH = 4
NSTEPS = 16
TICKS = 4
LAYERS = 4
TOKENS = 1024
ROWS = 1024
N_HEAD = 4


def draw_key_values(key, part):
    first = jax.random.fold_in(key, 0)
    shape = (LAYERS, 2, TOKENS, D)
    base = jnp.clip(jax.random.normal(first, shape, jnp.float32), -4.0, 4.0)
    return base.astype(jnp.bfloat16)


def with_ends(values, own_key, low, high):
    longest = values.shape.index(max(values.shape))
    spots = []
    for shift in (0, 1):
        where = [jax.random.randint(jax.random.fold_in(own_key, axis), (), 0, length) for axis, length in enumerate(values.shape)]
        where[longest] = (where[longest] + shift) % values.shape[longest]
        spots.append(tuple(where))
    return values.at[spots[0]].set(low).at[spots[1]].set(high)


def block_scale(rng, dims, cuts, least, top_value):
    level = 1.0
    for dim, shards_of in cuts:
        draws = jax.random.uniform(jax.random.fold_in(jax.random.fold_in(rng, 6), dim), (shards_of,), jnp.float32, least / len(cuts), top_value / len(cuts))
        level = level * jnp.repeat(jnp.exp(draws), dims[dim] // shards_of).reshape((-1,) + (1,) * (len(dims) - 1 - dim))
    return level


def gaussian(key, dims, deviation, most, shards=(), kind=jnp.bfloat16):
    entries = deviation * jax.random.normal(key, dims, jnp.float32)
    if shards:
        entries = entries * block_scale(key, dims, shards, -0.22, 0.18)
    return jnp.clip(entries, -most, most).astype(kind)


def setup_inputs(seed: int = 0, part: int = 0) -> dict:
    arg_keys = jax.random.split(jax.random.key(seed), 11)
    own_keys = jax.random.split(jax.random.fold_in(arg_keys[10], part), 11)
    hidden_in = gaussian(own_keys[0], (ROWS, D), 1.0, 6.0, ((0, 4), (1, 4)))
    latent_in = gaussian(own_keys[1], (ROWS, D), 1.0, 6.0, ((0, 4), (1, 4)))
    key_values = draw_key_values(jax.random.fold_in(jax.random.fold_in(arg_keys[10], part), 71), part)
    qkv_weight = gaussian(arg_keys[3], (LAYERS, D, 3, D), D ** -0.5, 0.109375, ((0, 4), (3, 4)))
    out_weight = gaussian(arg_keys[4], (LAYERS, D, D), D ** -0.5, 0.109375, ((0, 4), (1, 4)))
    modulation = gaussian(arg_keys[5], (LAYERS, NSTEPS, 3, D), 0.3, 1.5, ((0, 4),), jnp.float32)
    step_sizes = jnp.clip(jnp.exp(jax.random.uniform(arg_keys[6], (NSTEPS,), jnp.float32, math.log(0.25), math.log(2.0))), 0.25, 2.0)
    patch_order = jax.random.permutation(own_keys[7], NPATCH).astype(jnp.int32)
    tick_patch = with_ends(jax.random.randint(own_keys[8], (TICKS, LAYERS), 0, NPATCH), jax.random.fold_in(own_keys[8], 1), 0, NPATCH - 1).astype(jnp.int32)
    step_ids = with_ends(jax.random.randint(own_keys[9], (TICKS, LAYERS), 0, NSTEPS), jax.random.fold_in(own_keys[9], 1), 0, NSTEPS - 1).astype(jnp.int32)
    return dict(hidden_in=hidden_in, latent_in=latent_in, key_values=key_values, qkv_weight=qkv_weight, out_weight=out_weight, modulation=modulation, step_sizes=step_sizes, patch_order=patch_order, tick_patch=tick_patch, step_ids=step_ids)


def normalize(hidden_rows, shift_vec, scale_vec):
    values_f32 = hidden_rows.astype(jnp.float32)
    center = lax.optimization_barrier(jnp.mean(values_f32, axis=-1, keepdims=True))
    centered = values_f32 - center
    variance = lax.optimization_barrier(jnp.mean(centered * centered, axis=-1, keepdims=True))
    return (centered * lax.rsqrt(variance + 1e-06) * (1.0 + scale_vec) + shift_vec).astype(jnp.bfloat16)

def attend(queries, cached_keys, cached_values):
    scores = jnp.einsum('phd,lhd->hpl', queries.astype(jnp.float32), cached_keys.astype(jnp.float32)) * HEAD_DIM ** (-0.5)
    highest = lax.optimization_barrier(jnp.max(scores, axis=-1, keepdims=True))
    expo = jnp.exp(scores - highest)
    attention = (expo / lax.optimization_barrier(jnp.sum(expo, axis=-1, keepdims=True))).astype(jnp.bfloat16)
    head_out = jnp.einsum('hpl,lhd->phd', attention.astype(jnp.float32), cached_values.astype(jnp.float32))
    return head_out.astype(jnp.bfloat16).reshape(queries.shape[0], D)

def reference(hidden_in, latent_in, key_values, qkv_weight, out_weight, modulation, step_sizes, patch_order, tick_patch, step_ids):
    hidden = [hidden_in[layer * PATCH:(layer + 1) * PATCH] for layer in range(LAYERS)]
    latent = [latent_in[layer * PATCH:(layer + 1) * PATCH] for layer in range(LAYERS)]
    caches = [key_values[layer] for layer in range(LAYERS)]
    share_width = D // N_HEAD
    for tick_number in range(TICKS):
        sent_hidden = []
        sent_latent = []
        for layer in range(LAYERS):
            patch_index = patch_order[tick_patch[tick_number, layer]].astype(jnp.int32)
            step_index = step_ids[tick_number, layer].astype(jnp.int32)
            mods = modulation[layer, step_index]
            normed = normalize(hidden[layer], mods[0], mods[1])
            projected = jnp.dot(normed, qkv_weight[layer].reshape(D, 3 * D), preferred_element_type=jnp.float32)
            projected = projected.astype(jnp.bfloat16).reshape(PATCH, 3, D)
            fresh_rows = jnp.stack([projected[:, 1], projected[:, 2]])
            zero_index = jnp.zeros((), jnp.int32)
            layer_cache = lax.dynamic_update_slice(caches[layer], fresh_rows, (zero_index, (patch_index * PATCH).astype(jnp.int32), zero_index))
            caches[layer] = layer_cache
            head_out = attend(projected[:, 0].reshape(PATCH, HEADS, HEAD_DIM), layer_cache[0].reshape(TOKENS, HEADS, HEAD_DIM), layer_cache[1].reshape(TOKENS, HEADS, HEAD_DIM))
            partial_value = jnp.einsum('pgc,gcd->gpd', head_out.reshape(PATCH, N_HEAD, share_width).astype(jnp.float32), out_weight[layer].reshape(N_HEAD, share_width, D).astype(jnp.float32))
            attended = lax.optimization_barrier(jnp.sum(partial_value.astype(jnp.bfloat16).astype(jnp.float32), axis=0))
            updated = (hidden[layer].astype(jnp.float32) + (1.0 + mods[2]) * attended).astype(jnp.bfloat16)
            if layer == LAYERS - 1:
                advanced = (latent[layer].astype(jnp.float32) + step_sizes[step_index] * updated.astype(jnp.float32)).astype(jnp.bfloat16)
                sent_hidden.append(advanced)
                sent_latent.append(advanced)
            else:
                sent_hidden.append(updated)
                sent_latent.append(latent[layer])
        hidden = [sent_hidden[-1]] + sent_hidden[:-1]
        latent = [sent_latent[-1]] + sent_latent[:-1]
    return (jnp.concatenate(hidden, axis=0), jnp.concatenate(latent, axis=0))
```

```python
import functools

import jax
import jax.numpy as jnp
from jax import lax
from jax.experimental import pallas as pl
from jax.experimental.pallas import tpu as pltpu
from jax.sharding import PartitionSpec as P

HEAD_DIM = 64
LANES = 128
CHUNKS = 2
VMEM_BYTES = 24 << 20

IN_VMEM = pl.BlockSpec(memory_space=pltpu.VMEM)
IN_SMEM = pl.BlockSpec(memory_space=pltpu.SMEM)


def shifted(value, axis, steps):
    count = lax.axis_size(axis)
    pairs = [(source, (source + steps) % count) for source in range(count)]
    return lax.ppermute(value, axis, pairs)


def swapped(value, axis, bit):
    return lax.ppermute(value, axis, [(i, i ^ bit) for i in range(lax.axis_size(axis))])


def project_kernel(width, me_ref, x0, x1, x2, x3, mods, weight, q_out, k_out, v_out, normed):
    me = me_ref[0]
    shares = (x0, x1, x2, x3)
    rows = x0.shape[0]
    features = len(shares) * width
    total = jnp.zeros((rows, 1), jnp.float32)
    for share in shares:
        total += jnp.sum(share[...].astype(jnp.float32), axis=-1, keepdims=True)
    center = total / features
    squares = jnp.zeros((rows, 1), jnp.float32)
    for share in shares:
        centered = share[...].astype(jnp.float32) - center
        squares += jnp.sum(centered * centered, axis=-1, keepdims=True)
    inverse = lax.rsqrt(squares / features + 1e-06)
    for j, share in enumerate(shares):
        at = pl.multiple_of((me ^ j) * width, width)
        centered = share[...].astype(jnp.float32) - center
        shift = mods[0:1, pl.ds(at, width)]
        scale = mods[1:2, pl.ds(at, width)]
        normed[:, pl.ds(at, width)] = (centered * inverse * (1.0 + scale) + shift).astype(
            jnp.bfloat16
        )
    for third, out in ((1, k_out), (2, v_out), (0, q_out)):
        out[...] = jnp.dot(
            normed[...], weight[third], preferred_element_type=jnp.float32
        ).astype(jnp.bfloat16)


def project(me, shares, mods, weight):
    rows, width = shares[0].shape
    out = jax.ShapeDtypeStruct((rows, width), jnp.bfloat16)
    return pl.pallas_call(
        functools.partial(project_kernel, width),
        out_shape=(out,) * 3,
        in_specs=[IN_SMEM] + [IN_VMEM] * 6,
        out_specs=(IN_VMEM,) * 3,
        scratch_shapes=[pltpu.VMEM((rows, 4 * width), jnp.bfloat16)],
        compiler_params=pltpu.CompilerParams(vmem_limit_bytes=VMEM_BYTES),
        cost_estimate=pl.CostEstimate(
            flops=2 * rows * 12 * width * width, bytes_accessed=14 * rows * width, transcendentals=0
        ),
        name="project",
    )(me, *shares, mods, weight)


def attend_kernel(width, count, me_ref, *refs):
    queries = refs[:count]
    keys, values, weight, far, near, side, own, heads = refs[count:]
    me = me_ref[0]
    rows = sum(q.shape[0] for q in queries)
    low = lax.broadcasted_iota(jnp.int32, (rows, LANES), 1) < HEAD_DIM
    zero = jnp.zeros((rows, LANES), jnp.bfloat16)
    ones = jnp.ones((keys.shape[0], LANES), jnp.bfloat16)
    for at in range(0, width, LANES):
        cols = slice(at, at + LANES)
        query = jnp.concatenate([q[:, cols] for q in queries], axis=0) * jnp.bfloat16(
            HEAD_DIM**-0.5
        )
        both = jnp.concatenate(
            [jnp.where(low, query, zero), jnp.where(low, zero, query)], axis=0
        )
        scores = lax.dot_general(
            both, keys[:, cols], (((1,), (1,)), ((), ())), preferred_element_type=jnp.float32
        )
        highest = jnp.max(scores, axis=-1, keepdims=True)
        expo = jnp.exp(scores - highest).astype(jnp.bfloat16)
        mixed = jnp.dot(
            expo,
            jnp.concatenate([values[:, cols], ones], axis=1),
            preferred_element_type=jnp.float32,
        )
        out = mixed[:, :LANES] / mixed[:, LANES:]
        heads[:, cols] = jnp.where(low, out[:rows], out[rows:]).astype(jnp.bfloat16)
    for j, out in ((3, far), (2, near), (1, side), (0, own)):
        at = pl.multiple_of((me ^ j) * width, width)
        out[...] = jnp.dot(
            heads[...], weight[:, pl.ds(at, width)], preferred_element_type=jnp.float32
        ).astype(jnp.bfloat16)


def attend(me, queries, keys, values, weight):
    rows = sum(q.shape[0] for q in queries)
    tokens, width = keys.shape
    out = jax.ShapeDtypeStruct((rows, width), jnp.bfloat16)
    return pl.pallas_call(
        functools.partial(attend_kernel, width, len(queries)),
        out_shape=(out,) * 4,
        in_specs=[IN_SMEM] + [IN_VMEM] * (3 + len(queries)),
        out_specs=(IN_VMEM,) * 4,
        scratch_shapes=[pltpu.VMEM((rows, width), jnp.bfloat16)],
        compiler_params=pltpu.CompilerParams(vmem_limit_bytes=VMEM_BYTES),
        cost_estimate=pl.CostEstimate(
            flops=2 * rows * width * (8 * tokens + 4 * width),
            bytes_accessed=14 * rows * width,
            transcendentals=rows * tokens * width // HEAD_DIM,
        ),
        name="attend",
    )(me, *queries, keys, values, weight)


def picked(table, indices):
    positions = jnp.arange(table.shape[0], dtype=jnp.int32)
    hits = positions[None, :] == indices[:, None]
    return jnp.sum(jnp.where(hits, table[None, :], jnp.zeros_like(table)[None, :]), axis=1)


def local_fast(
    hidden_in,
    latent_in,
    key_values,
    qkv_weight,
    out_weight,
    modulation,
    step_sizes,
    patch_order,
    tick_patch,
    step_ids,
):
    segment_index = lax.axis_index("segment")
    sections = lax.axis_size("segment")
    last = sections - 1
    is_last = segment_index == last
    ticks = tick_patch.shape[0]
    rows, width = hidden_in.shape
    head_index = lax.axis_index("head").astype(jnp.int32)
    me = head_index.reshape(1)
    weight = jnp.transpose(qkv_weight[0], (1, 0, 2))
    projection = out_weight[0]
    keys, values = key_values[0, 0], key_values[0, 1]

    own_patch = lax.dynamic_index_in_dim(tick_patch, segment_index, 1, keepdims=False)
    own_step = lax.dynamic_index_in_dim(step_ids, segment_index, 1, keepdims=False)
    patches = picked(patch_order, own_patch)
    step_values = picked(step_sizes, own_step)
    last_step = picked(step_sizes, step_ids[ticks - 1, last :])[0]
    mods = [
        lax.dynamic_index_in_dim(modulation[0], own_step[k], 0, keepdims=False)
        for k in range(ticks)
    ]
    gates = [
        1.0 + lax.dynamic_slice_in_dim(mods[k][2], head_index * width, width, 0)
        for k in range(ticks)
    ]

    step_rows = rows // CHUNKS
    cuts = [slice(c * step_rows, (c + 1) * step_rows) for c in range(CHUNKS)]
    hidden = [hidden_in[cut] for cut in cuts]
    out_latent = None
    for k in range(ticks):
        latent = latent_in
        if 0 < k < last:
            latent = lax.ppermute(latent_in, "segment", [(last - k, last)])
        queries = []
        for cut, part in zip(cuts, hidden):
            across = swapped(part, "head", 2)
            beside = swapped(part, "head", 1)
            corner = swapped(across, "head", 1)
            query, fresh_keys, fresh_values = project(
                me, (part, beside, across, corner), mods[k], weight
            )
            queries.append(query)
            at = patches[k] * rows + cut.start
            keys = lax.dynamic_update_slice(keys, fresh_keys, (at, 0))
            values = lax.dynamic_update_slice(values, fresh_values, (at, 0))
        far, near, side, own = attend(me, queries, keys, values, projection)
        near_sum = (near.astype(jnp.float32) + swapped(far, "head", 1).astype(jnp.float32)).astype(
            jnp.bfloat16
        )
        side_in = swapped(side, "head", 1)
        advanced_parts = []
        sent = []
        for cut, part in zip(cuts, hidden):
            arrived = swapped(near_sum[cut], "head", 2)
            attended = (
                own[cut].astype(jnp.float32)
                + side_in[cut].astype(jnp.float32)
                + arrived.astype(jnp.float32)
            )
            updated = (part.astype(jnp.float32) + gates[k] * attended).astype(jnp.bfloat16)
            if k < ticks - 1:
                advanced = (
                    latent[cut].astype(jnp.float32)
                    + step_values[k] * updated.astype(jnp.float32)
                ).astype(jnp.bfloat16)
                advanced_parts.append(advanced)
                updated = jnp.where(is_last, advanced, updated)
            sent.append(shifted(updated, "segment", 1))
        hidden = sent
        if k < ticks - 1:
            done = jnp.concatenate(advanced_parts, axis=0)
            if k == 0:
                out_latent = done
            else:
                moved = lax.ppermute(done, "segment", [(last, last - k)])
                out_latent = jnp.where(segment_index == last - k, moved, out_latent)
    full = jnp.concatenate(hidden, axis=0)
    advanced = (
        latent_in.astype(jnp.float32) + last_step * full.astype(jnp.float32)
    ).astype(jnp.bfloat16)
    is_first = segment_index == 0
    return (jnp.where(is_first, advanced, full), jnp.where(is_first, advanced, out_latent))


def normalize(hidden_rows, shift_vec, scale_vec):
    values_f32 = hidden_rows.astype(jnp.float32)
    center = jnp.mean(values_f32, axis=-1, keepdims=True)
    centered = values_f32 - center
    variance = jnp.mean(centered * centered, axis=-1, keepdims=True)
    return (centered * lax.rsqrt(variance + 1e-06) * (1.0 + scale_vec) + shift_vec).astype(
        jnp.bfloat16
    )


def pick_value(table_row, index_value):
    positions = jnp.arange(table_row.shape[0], dtype=jnp.int32)
    return jnp.sum(jnp.where(positions == index_value, table_row, jnp.zeros_like(table_row)))


def local_general(
    hidden_in,
    latent_in,
    key_values,
    qkv_weight,
    out_weight,
    modulation,
    step_sizes,
    patch_order,
    tick_patch,
    step_ids,
):
    segment_index = lax.axis_index("segment")
    last_segment = lax.axis_size("segment") - 1
    local_width = out_weight.shape[1]
    model_width = out_weight.shape[2]
    column = lax.axis_index("head") * local_width
    heads_here = local_width // HEAD_DIM
    patch_rows = hidden_in.shape[0]
    weights_local = qkv_weight[0].reshape(model_width, 3 * local_width)
    projection = out_weight[0]
    step_table = modulation[0]
    layer_cache = key_values[0]
    tokens = layer_cache.shape[1]
    is_last = segment_index == last_segment
    part_hidden, part_latent = (hidden_in, latent_in)
    for tick_number in range(tick_patch.shape[0]):
        position = pick_value(tick_patch[tick_number], segment_index)
        patch_index = pick_value(patch_order, position)
        step_index = pick_value(step_ids[tick_number], segment_index)
        mods = lax.dynamic_index_in_dim(step_table, step_index, 0, keepdims=False)
        step_size = pick_value(step_sizes, step_index)
        patch_index, mods, step_size = (patch_index, mods, step_size)
        full_hidden = lax.all_gather(part_hidden, "head", axis=1, tiled=True)
        current_cache = layer_cache
        normed = normalize(full_hidden, mods[0], mods[1])
        projected = jnp.dot(normed, weights_local, preferred_element_type=jnp.float32)
        projected = projected.astype(jnp.bfloat16).reshape(patch_rows, 3, local_width)
        fresh_rows = jnp.stack([projected[:, 1], projected[:, 2]])
        zero_index = jnp.zeros((), jnp.int32)
        current_cache = lax.dynamic_update_slice(
            current_cache, fresh_rows, (zero_index, patch_index * patch_rows, zero_index)
        )
        queries = projected[:, 0].reshape(patch_rows, heads_here, HEAD_DIM)
        cached_keys = current_cache[0].reshape(tokens, heads_here, HEAD_DIM)
        cached_values = current_cache[1].reshape(tokens, heads_here, HEAD_DIM)
        scores = jnp.einsum(
            "phd,lhd->hpl", queries, cached_keys, preferred_element_type=jnp.float32
        ) * HEAD_DIM ** (-0.5)
        highest = jnp.max(scores, axis=-1, keepdims=True)
        expo = jnp.exp(scores - highest)
        attention = (expo / jnp.sum(expo, axis=-1, keepdims=True)).astype(jnp.bfloat16)
        head_out = jnp.einsum(
            "hpl,lhd->phd", attention, cached_values, preferred_element_type=jnp.float32
        )
        head_out = head_out.astype(jnp.bfloat16).reshape(patch_rows, local_width)
        partial_value = jnp.dot(head_out, projection, preferred_element_type=jnp.float32)
        partial_value, layer_cache = (partial_value, current_cache)
        attended = lax.psum_scatter(
            partial_value.astype(jnp.bfloat16), "head", scatter_dimension=1, tiled=True
        ).astype(jnp.float32)
        gate_cols = lax.dynamic_slice_in_dim(mods[2], column, local_width, 0)
        updated = (part_hidden.astype(jnp.float32) + (1.0 + gate_cols) * attended).astype(
            jnp.bfloat16
        )
        advanced = (
            part_latent.astype(jnp.float32) + step_size * updated.astype(jnp.float32)
        ).astype(jnp.bfloat16)
        send_hidden = jnp.where(is_last, advanced, updated)
        send_latent = jnp.where(is_last, advanced, part_latent)
        part_hidden, part_latent = shifted((send_hidden, send_latent), "segment", 1)
    return (part_hidden, part_latent)


def solution(mesh):
    shape = mesh.shape

    def local(*args):
        hidden_in, ticks = args[0], args[8].shape[0]
        fits = (
            shape["head"] == 4
            and hidden_in.shape[1] % LANES == 0
            and hidden_in.shape[0] % (16 * CHUNKS) == 0
            and ticks == shape["segment"]
            and ticks > 1
        )
        return local_fast(*args) if fits else local_general(*args)

    return jax.shard_map(
        local,
        mesh=mesh,
        in_specs=(
            P(("groups", "segment"), "head"),
            P(("groups", "segment"), "head"),
            P(("groups", "segment"), None, None, "head"),
            P("segment", None, None, "head"),
            P("segment", "head", None),
            P("segment", None, None, None),
            P(),
            P("groups"),
            P("groups", None),
            P("groups", None),
        ),
        out_specs=(P(("groups", "segment"), "head"), P(("groups", "segment"), "head")),
        check_vma=False,
    )
```

```python
import functools

import jax
import jax.numpy as jnp
from jax import lax
from jax.experimental import pallas as pl
from jax.experimental.pallas import tpu as pltpu
from jax.sharding import PartitionSpec as P

HEAD_DIM = 64
LANES = 128
CHUNKS = 2
VMEM_BYTES = 12 << 20

IN_VMEM = pl.BlockSpec(memory_space=pltpu.VMEM)
IN_SMEM = pl.BlockSpec(memory_space=pltpu.SMEM)
ANYWHERE = pl.BlockSpec(memory_space=pl.ANY)


def shifted(value, axis, steps):
    count = lax.axis_size(axis)
    pairs = [(source, (source + steps) % count) for source in range(count)]
    return lax.ppermute(value, axis, pairs)


def swapped(value, axis, bit):
    return lax.ppermute(value, axis, [(i, i ^ bit) for i in range(lax.axis_size(axis))])


def position(axis):
    return lax.axis_index(axis).astype(jnp.int32)


def project_kernel(
    width, tick, start, patch_rows, tick_patch, patch_order, step_ids, x0, x1, x2, x3, mods, weight,
    keys_in, values_in, q_out, keys_out, values_out, normed, k_new, v_new, sems,
):
    me, segment = position("head"), position("segment")
    step = step_ids[tick, segment]
    patch = patch_order[tick_patch[tick, segment]]
    shares = (x0, x1, x2, x3)
    rows = x0.shape[0]
    features = len(shares) * width
    total = jnp.zeros((rows, 1), jnp.float32)
    for share in shares:
        total += jnp.sum(share[...].astype(jnp.float32), axis=-1, keepdims=True)
    center = total / features
    squares = jnp.zeros((rows, 1), jnp.float32)
    for share in shares:
        centered = share[...].astype(jnp.float32) - center
        squares += jnp.sum(centered * centered, axis=-1, keepdims=True)
    inverse = lax.rsqrt(squares / features + 1e-06)
    for j, share in enumerate(shares):
        at = pl.multiple_of((me ^ j) * width, width)
        centered = share[...].astype(jnp.float32) - center
        shift = mods[0, pl.ds(step, 1), pl.ds(at, width)]
        scale = mods[1, pl.ds(step, 1), pl.ds(at, width)]
        normed[:, pl.ds(at, width)] = (centered * inverse * (1.0 + scale) + shift).astype(
            jnp.bfloat16
        )
    row = pl.multiple_of(patch * patch_rows + start, 16)
    copies = []
    for third, fresh, cache in ((1, k_new, keys_out), (2, v_new, values_out), (0, q_out, None)):
        fresh[...] = jnp.dot(
            normed[...], weight[third], preferred_element_type=jnp.float32
        ).astype(jnp.bfloat16)
        if cache is not None:
            copy = pltpu.make_async_copy(
                fresh, cache.at[pl.ds(row, rows), :], sems.at[third - 1]
            )
            copy.start()
            copies.append(copy)
    for copy in copies:
        copy.wait()


def project(tick, start, patch_rows, tables, shares, mods, weight, keys, values):
    rows, width = shares[0].shape
    block = pltpu.VMEM((rows, width), jnp.bfloat16)
    cache = jax.ShapeDtypeStruct(keys.shape, keys.dtype)
    return pl.pallas_call(
        functools.partial(project_kernel, width, tick, start, patch_rows),
        out_shape=(jax.ShapeDtypeStruct((rows, width), jnp.bfloat16), cache, cache),
        in_specs=[IN_SMEM] * 3 + [IN_VMEM] * 6 + [ANYWHERE] * 2,
        out_specs=(IN_VMEM, ANYWHERE, ANYWHERE),
        input_output_aliases={9: 1, 10: 2},
        scratch_shapes=[
            pltpu.VMEM((rows, 4 * width), jnp.bfloat16), block, block, pltpu.SemaphoreType.DMA((2,))
        ],
        compiler_params=pltpu.CompilerParams(vmem_limit_bytes=VMEM_BYTES),
        cost_estimate=pl.CostEstimate(
            flops=2 * rows * 12 * width * width, bytes_accessed=14 * rows * width, transcendentals=0
        ),
        name="project",
    )(*tables, *shares, mods, weight, keys, values)


def attend_kernel(width, count, extra, *refs):
    queries = refs[:count]
    keys, values, weight = refs[count : count + 3]
    far, near, side, own, heads = refs[count + 3 + extra :]
    me = position("head")
    rows = sum(q.shape[0] for q in queries)
    low = lax.broadcasted_iota(jnp.int32, (rows, LANES), 1) < HEAD_DIM
    zero = jnp.zeros((rows, LANES), jnp.bfloat16)
    ones = jnp.ones((keys.shape[0], LANES), jnp.bfloat16)
    for at in range(0, width, LANES):
        cols = slice(at, at + LANES)
        query = jnp.concatenate([q[:, cols] for q in queries], axis=0) * jnp.bfloat16(
            HEAD_DIM**-0.5
        )
        both = jnp.concatenate(
            [jnp.where(low, query, zero), jnp.where(low, zero, query)], axis=0
        )
        scores = lax.dot_general(
            both, keys[:, cols], (((1,), (1,)), ((), ())), preferred_element_type=jnp.float32
        )
        highest = jnp.max(scores, axis=-1, keepdims=True)
        expo = jnp.exp(scores - highest).astype(jnp.bfloat16)
        mixed = jnp.dot(
            expo,
            jnp.concatenate([values[:, cols], ones], axis=1),
            preferred_element_type=jnp.float32,
        )
        out = mixed[:, :LANES] / mixed[:, LANES:]
        heads[:, cols] = jnp.where(low, out[:rows], out[rows:]).astype(jnp.bfloat16)
    for j, out in ((3, far), (2, near), (1, side), (0, own)):
        at = pl.multiple_of((me ^ j) * width, width)
        out[...] = jnp.dot(
            heads[...], weight[:, pl.ds(at, width)], preferred_element_type=jnp.float32
        ).astype(jnp.bfloat16)


def attend(queries, keys, values, weight, arrived):
    rows = sum(q.shape[0] for q in queries)
    tokens, width = keys.shape
    out = jax.ShapeDtypeStruct((rows, width), jnp.bfloat16)
    return pl.pallas_call(
        functools.partial(attend_kernel, width, len(queries), len(arrived)),
        out_shape=(out,) * 4,
        in_specs=[IN_VMEM] * (3 + len(queries)) + [ANYWHERE] * len(arrived),
        out_specs=(IN_VMEM,) * 4,
        scratch_shapes=[pltpu.VMEM((rows, width), jnp.bfloat16)],
        compiler_params=pltpu.CompilerParams(vmem_limit_bytes=VMEM_BYTES),
        cost_estimate=pl.CostEstimate(
            flops=2 * rows * width * (8 * tokens + 4 * width),
            bytes_accessed=14 * rows * width,
            transcendentals=rows * tokens * width // HEAD_DIM,
        ),
        name="attend",
    )(*queries, keys, values, weight, *arrived)


def update_kernel(
    tick, start, step_ids, step_sizes, own, side, arrived, hidden, latent, mods, sent, advanced
):
    me, segment = position("head"), position("segment")
    rows, width = hidden.shape
    step = step_ids[tick, segment]
    cut = pl.ds(start, rows)
    attended = (
        own[cut, :].astype(jnp.float32)
        + side[cut, :].astype(jnp.float32)
        + arrived[...].astype(jnp.float32)
    )
    at = pl.multiple_of(me * width, width)
    gate = 1.0 + mods[2, pl.ds(step, 1), pl.ds(at, width)]
    updated = (hidden[...].astype(jnp.float32) + gate * attended).astype(jnp.bfloat16)
    sent[...] = updated
    if advanced is not None:
        moved = (
            latent[cut, :].astype(jnp.float32) + step_sizes[step] * updated.astype(jnp.float32)
        ).astype(jnp.bfloat16)
        advanced[...] = moved
        is_last = segment == lax.axis_size("segment") - 1

        @pl.when(is_last)
        def _():
            sent[...] = moved


def update(tick, start, tables, own, side, arrived, hidden, latent, mods):
    out = jax.ShapeDtypeStruct(hidden.shape, hidden.dtype)
    if latent is None:

        def body(*refs):
            update_kernel(tick, start, *refs[:6], None, *refs[6:8], None)

        arrays, outs = (own, side, arrived, hidden, mods), 1
    else:
        body = functools.partial(update_kernel, tick, start)
        arrays, outs = (own, side, arrived, hidden, latent, mods), 2
    return pl.pallas_call(
        body,
        out_shape=(out,) * outs,
        in_specs=[IN_SMEM] * 2 + [IN_VMEM] * len(arrays),
        out_specs=(IN_VMEM,) * outs,
        compiler_params=pltpu.CompilerParams(vmem_limit_bytes=VMEM_BYTES),
        cost_estimate=pl.CostEstimate(
            flops=8 * hidden.size, bytes_accessed=16 * hidden.size, transcendentals=0
        ),
        name="update",
    )(*tables, *arrays)


def finish_kernel(cuts, count, step_ids, step_sizes, latent, *refs):
    segment = position("segment")
    last = lax.axis_size("segment") - 1
    parts = refs[: len(cuts)]
    kept = refs[len(cuts) : 2 * len(cuts)]
    moved = refs[2 * len(cuts) : 2 * len(cuts) + count]
    out_hidden, out_latent = refs[2 * len(cuts) + count :]
    for cut, part, piece in zip(cuts, parts, kept):
        out_hidden[cut, :] = part[...]
        out_latent[cut, :] = piece[...]
    for k, array in enumerate(moved):

        @pl.when(segment == last - 1 - k)
        def _():
            out_latent[...] = array[...]

    @pl.when(segment == 0)
    def _():
        step_size = step_sizes[step_ids[step_ids.shape[0] - 1, last]]
        for cut, part in zip(cuts, parts):
            advanced = (
                latent[cut, :].astype(jnp.float32) + step_size * part[...].astype(jnp.float32)
            ).astype(jnp.bfloat16)
            out_hidden[cut, :] = advanced
            out_latent[cut, :] = advanced


def finish(cuts, tables, latent, parts, kept, moved):
    out = jax.ShapeDtypeStruct(latent.shape, latent.dtype)
    arrays = (latent, *parts, *kept, *moved)
    return pl.pallas_call(
        functools.partial(finish_kernel, cuts, len(moved)),
        out_shape=(out, out),
        in_specs=[IN_SMEM] * 2 + [IN_VMEM] * len(arrays),
        out_specs=(IN_VMEM, IN_VMEM),
        compiler_params=pltpu.CompilerParams(vmem_limit_bytes=VMEM_BYTES),
        name="finish",
    )(*tables, *arrays)


def local_fast(
    hidden_in,
    latent_in,
    key_values,
    qkv_weight,
    out_weight,
    modulation,
    step_sizes,
    patch_order,
    tick_patch,
    step_ids,
):
    last = lax.axis_size("segment") - 1
    ticks = tick_patch.shape[0]
    rows = hidden_in.shape[0]
    weight = jnp.transpose(qkv_weight[0], (1, 0, 2))
    mods = jnp.transpose(modulation[0], (1, 0, 2))
    projection = out_weight[0]
    keys, values = key_values[0, 0], key_values[0, 1]
    plan = (tick_patch, patch_order, step_ids)
    steps = (step_ids, step_sizes)

    step_rows = rows // CHUNKS
    cuts = [slice(c * step_rows, (c + 1) * step_rows) for c in range(CHUNKS)]
    hidden = [hidden_in[cut] for cut in cuts]
    latents = {0: latent_in}
    kept, moved = [], []
    for k in range(ticks):
        arrived = []
        if k + 1 < last:
            latents[k + 1] = lax.ppermute(latent_in, "segment", [(last - k - 1, last)])
            arrived.append(latents[k + 1])
        if moved:
            arrived.append(moved[-1])
        queries = []
        for cut, part in zip(cuts, hidden):
            across = swapped(part, "head", 2)
            beside = swapped(part, "head", 1)
            if queries:
                across, _ = lax.optimization_barrier((across, queries[-1]))
            corner = swapped(across, "head", 1)
            shares = (part, beside, across, corner)
            query, keys, values = project(
                k, cut.start, rows, plan, shares, mods, weight, keys, values
            )
            queries.append(query)
        far, near, side, own = attend(queries, keys, values, projection, arrived)
        far_in = swapped(far, "head", 1)
        side_in = swapped(side, "head", 1)
        advanced_parts = []
        sent = []
        for cut, part in zip(cuts, hidden):
            near_sum = (
                near[cut].astype(jnp.float32) + far_in[cut].astype(jnp.float32)
            ).astype(jnp.bfloat16)
            across = swapped(near_sum, "head", 2)
            latent = latents[k] if k < last else None
            onward, *advanced = update(
                k, cut.start, steps, own, side_in, across, part, latent, mods
            )
            advanced_parts += advanced
            sent.append(shifted(onward, "segment", 1))
        hidden = sent
        if k == 0:
            kept = advanced_parts
        elif k < last:
            done = jnp.concatenate(advanced_parts, axis=0)
            moved.append(lax.ppermute(done, "segment", [(last, last - k)]))
    return finish(cuts, steps, latent_in, hidden, kept, moved)


def normalize(hidden_rows, shift_vec, scale_vec):
    values_f32 = hidden_rows.astype(jnp.float32)
    center = jnp.mean(values_f32, axis=-1, keepdims=True)
    centered = values_f32 - center
    variance = jnp.mean(centered * centered, axis=-1, keepdims=True)
    return (centered * lax.rsqrt(variance + 1e-06) * (1.0 + scale_vec) + shift_vec).astype(
        jnp.bfloat16
    )


def pick_value(table_row, index_value):
    positions = jnp.arange(table_row.shape[0], dtype=jnp.int32)
    return jnp.sum(jnp.where(positions == index_value, table_row, jnp.zeros_like(table_row)))


def local_general(
    hidden_in,
    latent_in,
    key_values,
    qkv_weight,
    out_weight,
    modulation,
    step_sizes,
    patch_order,
    tick_patch,
    step_ids,
):
    segment_index = lax.axis_index("segment")
    last_segment = lax.axis_size("segment") - 1
    local_width = out_weight.shape[1]
    model_width = out_weight.shape[2]
    column = lax.axis_index("head") * local_width
    heads_here = local_width // HEAD_DIM
    patch_rows = hidden_in.shape[0]
    weights_local = qkv_weight[0].reshape(model_width, 3 * local_width)
    projection = out_weight[0]
    step_table = modulation[0]
    layer_cache = key_values[0]
    tokens = layer_cache.shape[1]
    is_last = segment_index == last_segment
    part_hidden, part_latent = (hidden_in, latent_in)
    for tick_number in range(tick_patch.shape[0]):
        position = pick_value(tick_patch[tick_number], segment_index)
        patch_index = pick_value(patch_order, position)
        step_index = pick_value(step_ids[tick_number], segment_index)
        mods = lax.dynamic_index_in_dim(step_table, step_index, 0, keepdims=False)
        step_size = pick_value(step_sizes, step_index)
        patch_index, mods, step_size = (patch_index, mods, step_size)
        full_hidden = lax.all_gather(part_hidden, "head", axis=1, tiled=True)
        current_cache = layer_cache
        normed = normalize(full_hidden, mods[0], mods[1])
        projected = jnp.dot(normed, weights_local, preferred_element_type=jnp.float32)
        projected = projected.astype(jnp.bfloat16).reshape(patch_rows, 3, local_width)
        fresh_rows = jnp.stack([projected[:, 1], projected[:, 2]])
        zero_index = jnp.zeros((), jnp.int32)
        current_cache = lax.dynamic_update_slice(
            current_cache, fresh_rows, (zero_index, patch_index * patch_rows, zero_index)
        )
        queries = projected[:, 0].reshape(patch_rows, heads_here, HEAD_DIM)
        cached_keys = current_cache[0].reshape(tokens, heads_here, HEAD_DIM)
        cached_values = current_cache[1].reshape(tokens, heads_here, HEAD_DIM)
        scores = jnp.einsum(
            "phd,lhd->hpl", queries, cached_keys, preferred_element_type=jnp.float32
        ) * HEAD_DIM ** (-0.5)
        highest = jnp.max(scores, axis=-1, keepdims=True)
        expo = jnp.exp(scores - highest)
        attention = (expo / jnp.sum(expo, axis=-1, keepdims=True)).astype(jnp.bfloat16)
        head_out = jnp.einsum(
            "hpl,lhd->phd", attention, cached_values, preferred_element_type=jnp.float32
        )
        head_out = head_out.astype(jnp.bfloat16).reshape(patch_rows, local_width)
        partial_value = jnp.dot(head_out, projection, preferred_element_type=jnp.float32)
        partial_value, layer_cache = (partial_value, current_cache)
        attended = lax.psum_scatter(
            partial_value.astype(jnp.bfloat16), "head", scatter_dimension=1, tiled=True
        ).astype(jnp.float32)
        gate_cols = lax.dynamic_slice_in_dim(mods[2], column, local_width, 0)
        updated = (part_hidden.astype(jnp.float32) + (1.0 + gate_cols) * attended).astype(
            jnp.bfloat16
        )
        advanced = (
            part_latent.astype(jnp.float32) + step_size * updated.astype(jnp.float32)
        ).astype(jnp.bfloat16)
        send_hidden = jnp.where(is_last, advanced, updated)
        send_latent = jnp.where(is_last, advanced, part_latent)
        part_hidden, part_latent = shifted((send_hidden, send_latent), "segment", 1)
    return (part_hidden, part_latent)


def solution(mesh):
    shape = mesh.shape

    def local(*args):
        hidden_in, ticks = args[0], args[8].shape[0]
        fits = (
            shape["head"] == 4
            and hidden_in.shape[1] % LANES == 0
            and hidden_in.shape[0] % (16 * CHUNKS) == 0
            and ticks == shape["segment"]
            and ticks > 1
        )
        return local_fast(*args) if fits else local_general(*args)

    return jax.shard_map(
        local,
        mesh=mesh,
        in_specs=(
            P(("groups", "segment"), "head"),
            P(("groups", "segment"), "head"),
            P(("groups", "segment"), None, None, "head"),
            P("segment", None, None, "head"),
            P("segment", "head", None),
            P("segment", None, None, None),
            P(),
            P("groups"),
            P("groups", None),
            P("groups", None),
        ),
        out_specs=(P(("groups", "segment"), "head"), P(("groups", "segment"), "head")),
        check_vma=False,
    )
```

```python
import functools

import jax
import jax.numpy as jnp
from jax import lax
from jax.experimental import pallas as pl
from jax.experimental.pallas import tpu as pltpu
from jax.sharding import PartitionSpec as P


HEAD_DIM = 64
LANES = 128
CHUNKS = 2
VMEM_BYTES = 12 << 20

IN_VMEM = pl.BlockSpec(memory_space=pltpu.VMEM)
ANYWHERE = pl.BlockSpec(memory_space=pl.ANY)


def shifted(value, axis, steps):
    count = lax.axis_size(axis)
    pairs = [(source, (source + steps) % count) for source in range(count)]
    return lax.ppermute(value, axis, pairs)


def swapped(value, axis, bit):
    return lax.ppermute(value, axis, [(i, i ^ bit) for i in range(lax.axis_size(axis))])


def position(axis):
    return lax.axis_index(axis).astype(jnp.int32)


def entry(row, index):
    row = row.astype(jnp.float32)
    hit = lax.broadcasted_iota(jnp.int32, row.shape, 1) == index
    return jnp.sum(jnp.where(hit, row, jnp.zeros_like(row)))


def whole(row, index):
    return entry(row, index).astype(jnp.int32)


def preload_kernel(weight, kept, sem):
    copy = pltpu.make_async_copy(weight, kept, sem)
    copy.start()
    copy.wait()


def preload(weight):
    return pl.pallas_call(
        preload_kernel,
        out_shape=pltpu.VMEM(weight.shape, weight.dtype),
        in_specs=[pl.BlockSpec(memory_space=pltpu.HBM)],
        out_specs=IN_VMEM,
        scratch_shapes=[pltpu.SemaphoreType.DMA],
        compiler_params=pltpu.CompilerParams(vmem_limit_bytes=VMEM_BYTES),
        cost_estimate=pl.CostEstimate(flops=0, bytes_accessed=4 * weight.size, transcendentals=0),
        name="preload",
    )(weight)


def project_kernel(width, tick, step_ids, x0, x1, x2, x3, mods, weight, q_out, k_out, v_out, normed):
    me, segment = position("head"), position("segment")
    step = whole(step_ids[tick : tick + 1, :], segment)
    shares = (x0, x1, x2, x3)
    rows = x0.shape[0]
    features = len(shares) * width
    total = jnp.zeros((rows, 1), jnp.float32)
    for share in shares:
        total += jnp.sum(share[...].astype(jnp.float32), axis=-1, keepdims=True)
    center = total / features
    squares = jnp.zeros((rows, 1), jnp.float32)
    for share in shares:
        centered = share[...].astype(jnp.float32) - center
        squares += jnp.sum(centered * centered, axis=-1, keepdims=True)
    inverse = lax.rsqrt(squares / features + 1e-06)
    for j, share in enumerate(shares):
        at = pl.multiple_of((me ^ j) * width, width)
        centered = share[...].astype(jnp.float32) - center
        shift = mods[0, pl.ds(step, 1), pl.ds(at, width)]
        scale = mods[1, pl.ds(step, 1), pl.ds(at, width)]
        normed[:, pl.ds(at, width)] = (centered * inverse * (1.0 + scale) + shift).astype(
            jnp.bfloat16
        )
    for third, out in ((1, k_out), (2, v_out), (0, q_out)):
        out[...] = jnp.dot(
            normed[...], weight[third], preferred_element_type=jnp.float32
        ).astype(jnp.bfloat16)


def project(tick, step_ids, shares, mods, weight):
    rows, width = shares[0].shape
    out = jax.ShapeDtypeStruct((rows, width), jnp.bfloat16)
    return pl.pallas_call(
        functools.partial(project_kernel, width, tick),
        out_shape=(out,) * 3,
        in_specs=[IN_VMEM] * 7,
        out_specs=(IN_VMEM,) * 3,
        scratch_shapes=[pltpu.VMEM((rows, 4 * width), jnp.bfloat16)],
        compiler_params=pltpu.CompilerParams(vmem_limit_bytes=VMEM_BYTES),
        cost_estimate=pl.CostEstimate(
            flops=2 * rows * 12 * width * width, bytes_accessed=14 * rows * width, transcendentals=0
        ),
        name="project",
    )(step_ids, *shares, mods, weight)


def attend_kernel(tick, chunks, extra, *refs):
    tick_patch, patch_order, old, weight = refs[:4]
    fresh = refs[4 : 4 + 3 * chunks]
    queries = fresh[0::3]
    far, near, heads, cache = refs[4 + 3 * chunks + extra :]
    me, segment = position("head"), position("segment")
    patch = whole(patch_order[...], whole(tick_patch[tick : tick + 1, :], segment))
    rows, width = heads.shape
    cache[...] = old[...]
    for i in range(2):
        start = 0
        for part in fresh[i + 1 :: 3]:
            at = pl.multiple_of(patch * rows + start, 16)
            cache[i, pl.ds(at, part.shape[0]), :] = part[...]
            start += part.shape[0]
    low = lax.broadcasted_iota(jnp.int32, (rows, LANES), 1) < HEAD_DIM
    zero = jnp.zeros((rows, LANES), jnp.bfloat16)
    ones = jnp.ones((cache.shape[1], LANES), jnp.bfloat16)
    for at in range(0, width, LANES):
        cols = slice(at, at + LANES)
        query = jnp.concatenate([q[:, cols] for q in queries], axis=0) * jnp.bfloat16(
            HEAD_DIM**-0.5
        )
        both = jnp.concatenate(
            [jnp.where(low, query, zero), jnp.where(low, zero, query)], axis=0
        )
        scores = lax.dot_general(
            both, cache[0, :, cols], (((1,), (1,)), ((), ())), preferred_element_type=jnp.float32
        )
        highest = jnp.max(scores, axis=-1, keepdims=True)
        expo = jnp.exp(scores - highest).astype(jnp.bfloat16)
        mixed = jnp.dot(
            expo,
            jnp.concatenate([cache[1, :, cols], ones], axis=1),
            preferred_element_type=jnp.float32,
        )
        out = mixed[:, :LANES] / mixed[:, LANES:]
        heads[:, cols] = jnp.where(low, out[:rows], out[rows:]).astype(jnp.bfloat16)
    for j, out in ((3, far), (2, near)):
        at = pl.multiple_of((me ^ j) * width, width)
        out[...] = jnp.dot(
            heads[...], weight[:, pl.ds(at, width)], preferred_element_type=jnp.float32
        ).astype(jnp.bfloat16)


def attend(tick, plan, fresh, cache, weight, arrived, final):
    rows = sum(query.shape[0] for query, _, _ in fresh)
    _, tokens, width = cache.shape
    out = jax.ShapeDtypeStruct((rows, width), jnp.bfloat16)
    kept = jax.ShapeDtypeStruct(cache.shape, cache.dtype)
    return pl.pallas_call(
        functools.partial(attend_kernel, tick, len(fresh), len(arrived)),
        out_shape=(out, out, out) + (() if final else (kept,)),
        in_specs=[IN_VMEM] * (4 + 3 * len(fresh)) + [ANYWHERE] * len(arrived),
        out_specs=(IN_VMEM,) * (3 if final else 4),
        scratch_shapes=[pltpu.VMEM(cache.shape, cache.dtype)] if final else [],
        compiler_params=pltpu.CompilerParams(vmem_limit_bytes=VMEM_BYTES),
        cost_estimate=pl.CostEstimate(
            flops=2 * rows * width * (8 * tokens + 2 * width),
            bytes_accessed=14 * rows * width,
            transcendentals=rows * tokens * width // HEAD_DIM,
        ),
        name="attend",
    )(*plan, cache, weight, *[array for part in fresh for array in part], *arrived)


def output_kernel(heads, weight, side, own):
    me = position("head")
    width = heads.shape[1]
    for j, out in ((1, side), (0, own)):
        at = pl.multiple_of((me ^ j) * width, width)
        out[...] = jnp.dot(
            heads[...], weight[:, pl.ds(at, width)], preferred_element_type=jnp.float32
        ).astype(jnp.bfloat16)


def output(heads, weight):
    out = jax.ShapeDtypeStruct(heads.shape, heads.dtype)
    return pl.pallas_call(
        output_kernel,
        out_shape=(out, out),
        in_specs=[IN_VMEM] * 2,
        out_specs=(IN_VMEM, IN_VMEM),
        compiler_params=pltpu.CompilerParams(vmem_limit_bytes=VMEM_BYTES),
        cost_estimate=pl.CostEstimate(
            flops=4 * heads.size * heads.shape[1], bytes_accessed=6 * heads.size, transcendentals=0
        ),
        name="output",
    )(heads, weight)


def update_kernel(
    tick, start, step_ids, step_sizes, own, side, arrived, hidden, latent, mods, sent, advanced
):
    me, segment = position("head"), position("segment")
    rows, width = hidden.shape
    step = whole(step_ids[tick : tick + 1, :], segment)
    cut = pl.ds(start, rows)
    attended = (
        own[cut, :].astype(jnp.float32)
        + side[cut, :].astype(jnp.float32)
        + arrived[...].astype(jnp.float32)
    )
    at = pl.multiple_of(me * width, width)
    gate = 1.0 + mods[2, pl.ds(step, 1), pl.ds(at, width)]
    updated = (hidden[...].astype(jnp.float32) + gate * attended).astype(jnp.bfloat16)
    sent[...] = updated
    if advanced is not None:
        moved = (
            latent[cut, :].astype(jnp.float32) + entry(step_sizes[...], step) * updated.astype(jnp.float32)
        ).astype(jnp.bfloat16)
        advanced[...] = moved
        is_last = segment == lax.axis_size("segment") - 1

        @pl.when(is_last)
        def _():
            sent[...] = moved


def update(tick, start, tables, own, side, arrived, hidden, latent, mods):
    out = jax.ShapeDtypeStruct(hidden.shape, hidden.dtype)
    if latent is None:

        def body(*refs):
            update_kernel(tick, start, *refs[:6], None, *refs[6:8], None)

        arrays, outs = (own, side, arrived, hidden, mods), 1
    else:
        body = functools.partial(update_kernel, tick, start)
        arrays, outs = (own, side, arrived, hidden, latent, mods), 2
    return pl.pallas_call(
        body,
        out_shape=(out,) * outs,
        in_specs=[IN_VMEM] * (2 + len(arrays)),
        out_specs=(IN_VMEM,) * outs,
        compiler_params=pltpu.CompilerParams(vmem_limit_bytes=VMEM_BYTES),
        cost_estimate=pl.CostEstimate(
            flops=8 * hidden.size, bytes_accessed=16 * hidden.size, transcendentals=0
        ),
        name="update",
    )(*tables, *arrays)


def finish_kernel(cuts, count, step_ids, step_sizes, latent, *refs):
    segment = position("segment")
    last = lax.axis_size("segment") - 1
    parts = refs[: len(cuts)]
    kept = refs[len(cuts) : 2 * len(cuts)]
    moved = refs[2 * len(cuts) : 2 * len(cuts) + count]
    out_hidden, out_latent = refs[2 * len(cuts) + count :]
    for cut, part, piece in zip(cuts, parts, kept):
        out_hidden[cut, :] = part[...]
        out_latent[cut, :] = piece[...]
    for k, array in enumerate(moved):

        @pl.when(segment == last - 1 - k)
        def _():
            out_latent[...] = array[...]

    @pl.when(segment == 0)
    def _():
        step_size = entry(step_sizes[...], whole(step_ids[step_ids.shape[0] - 1 :, :], last))
        for cut, part in zip(cuts, parts):
            advanced = (
                latent[cut, :].astype(jnp.float32) + step_size * part[...].astype(jnp.float32)
            ).astype(jnp.bfloat16)
            out_hidden[cut, :] = advanced
            out_latent[cut, :] = advanced


def finish(cuts, tables, latent, parts, kept, moved):
    out = jax.ShapeDtypeStruct(latent.shape, latent.dtype)
    arrays = (latent, *parts, *kept, *moved)
    return pl.pallas_call(
        functools.partial(finish_kernel, cuts, len(moved)),
        out_shape=(out, out),
        in_specs=[IN_VMEM] * (2 + len(arrays)),
        out_specs=(IN_VMEM, IN_VMEM),
        compiler_params=pltpu.CompilerParams(vmem_limit_bytes=VMEM_BYTES),
        name="finish",
    )(*tables, *arrays)


def local_fast(
    hidden_in,
    latent_in,
    key_values,
    qkv_weight,
    out_weight,
    modulation,
    step_sizes,
    patch_order,
    tick_patch,
    step_ids,
):
    last = lax.axis_size("segment") - 1
    ticks = tick_patch.shape[0]
    rows = hidden_in.shape[0]
    weight = jnp.transpose(qkv_weight[0], (1, 0, 2))
    mods = jnp.transpose(modulation[0], (1, 0, 2))
    projection = out_weight[0]
    weight = preload(weight)
    cache = key_values[0]
    plan = (tick_patch, patch_order.reshape(1, -1))
    steps = (step_ids, step_sizes.reshape(1, -1))

    step_rows = rows // CHUNKS
    cuts = [slice(c * step_rows, (c + 1) * step_rows) for c in range(CHUNKS)]
    hidden = [hidden_in[cut] for cut in cuts]
    latents = {0: latent_in}
    for k in range(1, last):
        latents[k] = lax.ppermute(latent_in, "segment", [(last - k, last)])
    kept, moved = [], []
    done = None
    for k in range(ticks):
        if done is not None:
            moved.append(lax.ppermute(done, "segment", [(last, last + 1 - k)]))
            done = None
        fresh = []
        for part in hidden:
            across = swapped(part, "head", 2)
            beside = swapped(part, "head", 1)
            if fresh:
                across, _ = lax.optimization_barrier((across, fresh[-1][0]))
            corner = swapped(across, "head", 1)
            fresh.append(
                project(k, step_ids, (part, beside, across, corner), mods, weight)
            )
        arrived = moved[:-1]
        far, near, heads, *rest = attend(k, plan, fresh, cache, projection, arrived, k == ticks - 1)
        if rest:
            cache = rest[0]
        far_in = swapped(far, "head", 1)
        sums = [
            (near[cut].astype(jnp.float32) + far_in[cut].astype(jnp.float32)).astype(jnp.bfloat16)
            for cut in cuts
        ]
        crossed = []
        for c in range(CHUNKS):
            crossed.append(swapped(sums[c], "head", 2))
        side, own = output(heads, projection)
        side_in = swapped(side, "head", 1)
        advanced_parts = []
        sent = []
        for c, part in enumerate(hidden):
            latent = latents[k] if k < last else None
            onward, *advanced = update(
                k, cuts[c].start, steps, own, side_in, crossed[c], part, latent, mods
            )
            advanced_parts += advanced
            sent.append(shifted(onward, "segment", 1))
        hidden = sent
        if k == 0:
            kept = advanced_parts
        elif k < last:
            done = jnp.concatenate(advanced_parts, axis=0)
    return finish(cuts, steps, latent_in, hidden, kept, moved)


def normalize(hidden_rows, shift_vec, scale_vec):
    values_f32 = hidden_rows.astype(jnp.float32)
    center = jnp.mean(values_f32, axis=-1, keepdims=True)
    centered = values_f32 - center
    variance = jnp.mean(centered * centered, axis=-1, keepdims=True)
    return (centered * lax.rsqrt(variance + 1e-06) * (1.0 + scale_vec) + shift_vec).astype(
        jnp.bfloat16
    )


def pick_value(table_row, index_value):
    positions = jnp.arange(table_row.shape[0], dtype=jnp.int32)
    return jnp.sum(jnp.where(positions == index_value, table_row, jnp.zeros_like(table_row)))


def local_general(
    hidden_in,
    latent_in,
    key_values,
    qkv_weight,
    out_weight,
    modulation,
    step_sizes,
    patch_order,
    tick_patch,
    step_ids,
):
    segment_index = lax.axis_index("segment")
    last_segment = lax.axis_size("segment") - 1
    local_width = out_weight.shape[1]
    model_width = out_weight.shape[2]
    column = lax.axis_index("head") * local_width
    heads_here = local_width // HEAD_DIM
    patch_rows = hidden_in.shape[0]
    weights_local = qkv_weight[0].reshape(model_width, 3 * local_width)
    projection = out_weight[0]
    step_table = modulation[0]
    layer_cache = key_values[0]
    tokens = layer_cache.shape[1]
    is_last = segment_index == last_segment
    part_hidden, part_latent = (hidden_in, latent_in)
    for tick_number in range(tick_patch.shape[0]):
        position = pick_value(tick_patch[tick_number], segment_index)
        patch_index = pick_value(patch_order, position)
        step_index = pick_value(step_ids[tick_number], segment_index)
        mods = lax.dynamic_index_in_dim(step_table, step_index, 0, keepdims=False)
        step_size = pick_value(step_sizes, step_index)
        patch_index, mods, step_size = (patch_index, mods, step_size)
        full_hidden = lax.all_gather(part_hidden, "head", axis=1, tiled=True)
        current_cache = layer_cache
        normed = normalize(full_hidden, mods[0], mods[1])
        projected = jnp.dot(normed, weights_local, preferred_element_type=jnp.float32)
        projected = projected.astype(jnp.bfloat16).reshape(patch_rows, 3, local_width)
        fresh_rows = jnp.stack([projected[:, 1], projected[:, 2]])
        zero_index = jnp.zeros((), jnp.int32)
        current_cache = lax.dynamic_update_slice(
            current_cache, fresh_rows, (zero_index, patch_index * patch_rows, zero_index)
        )
        queries = projected[:, 0].reshape(patch_rows, heads_here, HEAD_DIM)
        cached_keys = current_cache[0].reshape(tokens, heads_here, HEAD_DIM)
        cached_values = current_cache[1].reshape(tokens, heads_here, HEAD_DIM)
        scores = jnp.einsum(
            "phd,lhd->hpl", queries, cached_keys, preferred_element_type=jnp.float32
        ) * HEAD_DIM ** (-0.5)
        highest = jnp.max(scores, axis=-1, keepdims=True)
        expo = jnp.exp(scores - highest)
        attention = (expo / jnp.sum(expo, axis=-1, keepdims=True)).astype(jnp.bfloat16)
        head_out = jnp.einsum(
            "hpl,lhd->phd", attention, cached_values, preferred_element_type=jnp.float32
        )
        head_out = head_out.astype(jnp.bfloat16).reshape(patch_rows, local_width)
        partial_value = jnp.dot(head_out, projection, preferred_element_type=jnp.float32)
        partial_value, layer_cache = (partial_value, current_cache)
        attended = lax.psum_scatter(
            partial_value.astype(jnp.bfloat16), "head", scatter_dimension=1, tiled=True
        ).astype(jnp.float32)
        gate_cols = lax.dynamic_slice_in_dim(mods[2], column, local_width, 0)
        updated = (part_hidden.astype(jnp.float32) + (1.0 + gate_cols) * attended).astype(
            jnp.bfloat16
        )
        advanced = (
            part_latent.astype(jnp.float32) + step_size * updated.astype(jnp.float32)
        ).astype(jnp.bfloat16)
        send_hidden = jnp.where(is_last, advanced, updated)
        send_latent = jnp.where(is_last, advanced, part_latent)
        part_hidden, part_latent = shifted((send_hidden, send_latent), "segment", 1)
    return (part_hidden, part_latent)


def solution(mesh):
    shape = mesh.shape

    def local(*args):
        hidden_in, ticks = args[0], args[8].shape[0]
        fits = (
            shape["head"] == 4
            and hidden_in.shape[1] % LANES == 0
            and hidden_in.shape[0] % (16 * CHUNKS) == 0
            and ticks == shape["segment"]
            and ticks > 1
        )
        return local_fast(*args) if fits else local_general(*args)

    return jax.shard_map(
        local,
        mesh=mesh,
        in_specs=(
            P(("groups", "segment"), "head"),
            P(("groups", "segment"), "head"),
            P(("groups", "segment"), None, None, "head"),
            P("segment", None, None, "head"),
            P("segment", "head", None),
            P("segment", None, None, None),
            P(),
            P("groups"),
            P("groups", None),
            P("groups", None),
        ),
        out_specs=(P(("groups", "segment"), "head"), P(("groups", "segment"), "head")),
        check_vma=False,
    )
```

```python
import functools

import jax
import jax.numpy as jnp
from jax import lax
from jax.experimental import pallas as pl
from jax.experimental.pallas import tpu as pltpu
from jax.sharding import PartitionSpec as P


HEAD_DIM = 64
LANES = 128
CHUNKS = 2
VMEM_BYTES = 12 << 20

IN_VMEM = pl.BlockSpec(memory_space=pltpu.VMEM)
ANYWHERE = pl.BlockSpec(memory_space=pl.ANY)


def shifted(value, axis, steps):
    count = lax.axis_size(axis)
    pairs = [(source, (source + steps) % count) for source in range(count)]
    return lax.ppermute(value, axis, pairs)


def swapped(value, axis, bit):
    return lax.ppermute(value, axis, [(i, i ^ bit) for i in range(lax.axis_size(axis))])


def position(axis):
    return lax.axis_index(axis).astype(jnp.int32)


def entry(row, index):
    row = row.astype(jnp.float32)
    hit = lax.broadcasted_iota(jnp.int32, row.shape, 1) == index
    return jnp.sum(jnp.where(hit, row, jnp.zeros_like(row)))


def whole(row, index):
    return entry(row, index).astype(jnp.int32)


def preload_kernel(weight, kept, sem):
    copy = pltpu.make_async_copy(weight, kept, sem)
    copy.start()
    copy.wait()


def preload(weight):
    return pl.pallas_call(
        preload_kernel,
        out_shape=pltpu.VMEM(weight.shape, weight.dtype),
        in_specs=[pl.BlockSpec(memory_space=pltpu.HBM)],
        out_specs=IN_VMEM,
        scratch_shapes=[pltpu.SemaphoreType.DMA],
        compiler_params=pltpu.CompilerParams(vmem_limit_bytes=VMEM_BYTES),
        cost_estimate=pl.CostEstimate(flops=0, bytes_accessed=4 * weight.size, transcendentals=0),
        name="preload",
    )(weight)


def project_kernel(width, tick, step_ids, x0, x1, x2, x3, mods, weight, q_out, k_out, v_out, normed):
    me, segment = position("head"), position("segment")
    step = whole(step_ids[tick : tick + 1, :], segment)
    shares = (x0, x1, x2, x3)
    rows = x0.shape[0]
    features = len(shares) * width
    total = jnp.zeros((rows, 1), jnp.float32)
    for share in shares:
        total += jnp.sum(share[...].astype(jnp.float32), axis=-1, keepdims=True)
    center = total / features
    squares = jnp.zeros((rows, 1), jnp.float32)
    for share in shares:
        centered = share[...].astype(jnp.float32) - center
        squares += jnp.sum(centered * centered, axis=-1, keepdims=True)
    inverse = lax.rsqrt(squares / features + 1e-06)
    for j, share in enumerate(shares):
        at = pl.multiple_of((me ^ j) * width, width)
        centered = share[...].astype(jnp.float32) - center
        shift = mods[0, pl.ds(step, 1), pl.ds(at, width)]
        scale = mods[1, pl.ds(step, 1), pl.ds(at, width)]
        normed[:, pl.ds(at, width)] = (centered * inverse * (1.0 + scale) + shift).astype(
            jnp.bfloat16
        )
    for third, out in ((1, k_out), (2, v_out), (0, q_out)):
        out[...] = jnp.dot(
            normed[...], weight[third], preferred_element_type=jnp.float32
        ).astype(jnp.bfloat16)


def project(tick, step_ids, shares, mods, weight):
    rows, width = shares[0].shape
    out = jax.ShapeDtypeStruct((rows, width), jnp.bfloat16)
    return pl.pallas_call(
        functools.partial(project_kernel, width, tick),
        out_shape=(out,) * 3,
        in_specs=[IN_VMEM] * 7,
        out_specs=(IN_VMEM,) * 3,
        scratch_shapes=[pltpu.VMEM((rows, 4 * width), jnp.bfloat16)],
        compiler_params=pltpu.CompilerParams(vmem_limit_bytes=VMEM_BYTES),
        cost_estimate=pl.CostEstimate(
            flops=2 * rows * 12 * width * width, bytes_accessed=14 * rows * width, transcendentals=0
        ),
        name="project",
    )(step_ids, *shares, mods, weight)


def attend_kernel(tick, chunks, extra, *refs):
    tick_patch, patch_order, old, weight = refs[:4]
    fresh = refs[4 : 4 + 3 * chunks]
    queries = fresh[0::3]
    far, heads, cache, even, odd = refs[4 + 3 * chunks + extra :]
    me, segment = position("head"), position("segment")
    patch = whole(patch_order[...], whole(tick_patch[tick : tick + 1, :], segment))
    rows, width = heads.shape

    @pl.loop(0, cache.shape[1] // rows)
    def _(block):
        cut = pl.ds(pl.multiple_of(block * rows, rows), rows)
        cache[:, cut, :] = old[:, cut, :]

    for i in range(2):
        start = 0
        for part in fresh[i + 1 :: 3]:
            at = pl.multiple_of(patch * rows + start, 16)
            cache[i, pl.ds(at, part.shape[0]), :] = part[...]
            start += part.shape[0]
    low = lax.broadcasted_iota(jnp.int32, (rows, LANES), 1) < HEAD_DIM
    zero = jnp.zeros((rows, LANES), jnp.bfloat16)
    ones = jnp.ones((cache.shape[1], LANES), jnp.bfloat16)

    def columns(pair):
        return pl.ds(pl.multiple_of(pair * LANES, LANES), LANES)

    def score(pair, scores):
        cols = columns(pair)
        query = jnp.concatenate([q[:, cols] for q in queries], axis=0) * jnp.bfloat16(
            HEAD_DIM**-0.5
        )
        both = jnp.concatenate(
            [jnp.where(low, query, zero), jnp.where(low, zero, query)], axis=0
        )
        scores[...] = lax.dot_general(
            both,
            cache[0, :, cols],
            (((1,), (1,)), ((), ())),
            preferred_element_type=jnp.float32,
        )

    def mix(pair, scores):
        cols = columns(pair)
        highest = jnp.max(scores[...], axis=-1, keepdims=True)
        expo = jnp.exp(scores[...] - highest).astype(jnp.bfloat16)
        mixed = jnp.dot(
            expo,
            jnp.concatenate([cache[1, :, cols], ones], axis=1),
            preferred_element_type=jnp.float32,
        )
        out = mixed[:, :LANES] / mixed[:, LANES:]
        heads[:, cols] = jnp.where(low, out[:rows], out[rows:]).astype(jnp.bfloat16)

    pairs = width // LANES
    score(0, even)

    @pl.loop(0, pairs // 2)
    def _(i):
        score(2 * i + 1, odd)
        mix(2 * i, even)
        score(jnp.minimum(2 * i + 2, pairs - 1), even)
        mix(2 * i + 1, odd)

    if pairs % 2:
        mix(pairs - 1, even)
    at = pl.multiple_of((me ^ 3) * width, width)
    far[...] = jnp.dot(
        heads[...], weight[:, pl.ds(at, width)], preferred_element_type=jnp.float32
    ).astype(jnp.bfloat16)


def attend(tick, plan, fresh, cache, weight, arrived, final):
    rows = sum(query.shape[0] for query, _, _ in fresh)
    _, tokens, width = cache.shape
    out = jax.ShapeDtypeStruct((rows, width), jnp.bfloat16)
    kept = jax.ShapeDtypeStruct(cache.shape, cache.dtype)
    return pl.pallas_call(
        functools.partial(attend_kernel, tick, len(fresh), len(arrived)),
        out_shape=(out, out) + (() if final else (kept,)),
        in_specs=[IN_VMEM] * (4 + 3 * len(fresh)) + [ANYWHERE] * len(arrived),
        out_specs=(IN_VMEM,) * (2 if final else 3),
        scratch_shapes=([pltpu.VMEM(cache.shape, cache.dtype)] if final else [])
        + [pltpu.VMEM((2 * rows, tokens), jnp.float32)] * 2,
        compiler_params=pltpu.CompilerParams(vmem_limit_bytes=VMEM_BYTES),
        cost_estimate=pl.CostEstimate(
            flops=2 * rows * width * (8 * tokens + 2 * width),
            bytes_accessed=14 * rows * width,
            transcendentals=rows * tokens * width // HEAD_DIM,
        ),
        name="attend",
    )(*plan, cache, weight, *[array for part in fresh for array in part], *arrived)


def output_kernel(heads, weight, out):
    me = position("head")
    width = heads.shape[1]

    @pl.loop(0, out.shape[0])
    def _(j):
        at = pl.multiple_of((me ^ j) * width, width)
        out[j] = jnp.dot(
            heads[...], weight[:, pl.ds(at, width)], preferred_element_type=jnp.float32
        ).astype(jnp.bfloat16)


def output(heads, weight):
    return pl.pallas_call(
        output_kernel,
        out_shape=jax.ShapeDtypeStruct((3,) + heads.shape, heads.dtype),
        in_specs=[IN_VMEM] * 2,
        out_specs=IN_VMEM,
        compiler_params=pltpu.CompilerParams(vmem_limit_bytes=VMEM_BYTES),
        cost_estimate=pl.CostEstimate(
            flops=6 * heads.size * heads.shape[1], bytes_accessed=6 * heads.size, transcendentals=0
        ),
        name="output",
    )(heads, weight)


def update_kernel(
    tick, start, step_ids, step_sizes, own, side, arrived, hidden, latent, mods, sent, advanced
):
    me, segment = position("head"), position("segment")
    rows, width = hidden.shape
    step = whole(step_ids[tick : tick + 1, :], segment)
    cut = pl.ds(start, rows)
    attended = (
        own[cut, :].astype(jnp.float32)
        + side[cut, :].astype(jnp.float32)
        + arrived[...].astype(jnp.float32)
    )
    at = pl.multiple_of(me * width, width)
    gate = 1.0 + mods[2, pl.ds(step, 1), pl.ds(at, width)]
    updated = (hidden[...].astype(jnp.float32) + gate * attended).astype(jnp.bfloat16)
    sent[...] = updated
    if advanced is not None:
        moved = (
            latent[cut, :].astype(jnp.float32) + entry(step_sizes[...], step) * updated.astype(jnp.float32)
        ).astype(jnp.bfloat16)
        advanced[...] = moved
        is_last = segment == lax.axis_size("segment") - 1

        @pl.when(is_last)
        def _():
            sent[...] = moved


def update(tick, start, tables, own, side, arrived, hidden, latent, mods):
    out = jax.ShapeDtypeStruct(hidden.shape, hidden.dtype)
    if latent is None:

        def body(*refs):
            update_kernel(tick, start, *refs[:6], None, *refs[6:8], None)

        arrays, outs = (own, side, arrived, hidden, mods), 1
    else:
        body = functools.partial(update_kernel, tick, start)
        arrays, outs = (own, side, arrived, hidden, latent, mods), 2
    return pl.pallas_call(
        body,
        out_shape=(out,) * outs,
        in_specs=[IN_VMEM] * (2 + len(arrays)),
        out_specs=(IN_VMEM,) * outs,
        compiler_params=pltpu.CompilerParams(vmem_limit_bytes=VMEM_BYTES),
        cost_estimate=pl.CostEstimate(
            flops=8 * hidden.size, bytes_accessed=16 * hidden.size, transcendentals=0
        ),
        name="update",
    )(*tables, *arrays)


def finish_kernel(cuts, count, step_ids, step_sizes, latent, *refs):
    segment = position("segment")
    last = lax.axis_size("segment") - 1
    parts = refs[: len(cuts)]
    kept = refs[len(cuts) : 2 * len(cuts)]
    moved = refs[2 * len(cuts) : 2 * len(cuts) + count]
    out_hidden, out_latent = refs[2 * len(cuts) + count :]
    for cut, part, piece in zip(cuts, parts, kept):
        out_hidden[cut, :] = part[...]
        out_latent[cut, :] = piece[...]
    for k, array in enumerate(moved):

        @pl.when(segment == last - 1 - k)
        def _():
            out_latent[...] = array[...]

    @pl.when(segment == 0)
    def _():
        step_size = entry(step_sizes[...], whole(step_ids[step_ids.shape[0] - 1 :, :], last))
        for cut, part in zip(cuts, parts):
            advanced = (
                latent[cut, :].astype(jnp.float32) + step_size * part[...].astype(jnp.float32)
            ).astype(jnp.bfloat16)
            out_hidden[cut, :] = advanced
            out_latent[cut, :] = advanced


def finish(cuts, tables, latent, parts, kept, moved):
    out = jax.ShapeDtypeStruct(latent.shape, latent.dtype)
    arrays = (latent, *parts, *kept, *moved)
    return pl.pallas_call(
        functools.partial(finish_kernel, cuts, len(moved)),
        out_shape=(out, out),
        in_specs=[IN_VMEM] * (2 + len(arrays)),
        out_specs=(IN_VMEM, IN_VMEM),
        compiler_params=pltpu.CompilerParams(vmem_limit_bytes=VMEM_BYTES),
        name="finish",
    )(*tables, *arrays)


def local_fast(
    hidden_in,
    latent_in,
    key_values,
    qkv_weight,
    out_weight,
    modulation,
    step_sizes,
    patch_order,
    tick_patch,
    step_ids,
):
    last = lax.axis_size("segment") - 1
    ticks = tick_patch.shape[0]
    rows = hidden_in.shape[0]
    weight = jnp.transpose(qkv_weight[0], (1, 0, 2))
    mods = jnp.transpose(modulation[0], (1, 0, 2))
    projection = out_weight[0]
    weight = preload(weight)
    cache = key_values[0]
    plan = (tick_patch, patch_order.reshape(1, -1))
    steps = (step_ids, step_sizes.reshape(1, -1))

    step_rows = rows // CHUNKS
    cuts = [slice(c * step_rows, (c + 1) * step_rows) for c in range(CHUNKS)]
    hidden = [hidden_in[cut] for cut in cuts]
    latents = {0: latent_in}
    kept, moved = [], []
    done = None
    for k in range(ticks):
        if done is not None:
            moved.append(lax.ppermute(done, "segment", [(last, last + 1 - k)]))
            done = None
        if k + 1 < last:
            latents[k + 1] = lax.ppermute(latent_in, "segment", [(last - k - 1, last)])
        fresh = []
        for part in hidden:
            across = swapped(part, "head", 2)
            beside = swapped(part, "head", 1)
            if fresh:
                across, _ = lax.optimization_barrier((across, fresh[-1][0]))
            corner = swapped(across, "head", 1)
            fresh.append(
                project(k, step_ids, (part, beside, across, corner), mods, weight)
            )
        arrived = moved[:-1]
        far, heads, *rest = attend(k, plan, fresh, cache, projection, arrived, k == ticks - 1)
        if rest:
            cache = rest[0]
        far_in = swapped(far, "head", 1)
        own, side, near = output(heads, projection)
        side_in = swapped(side, "head", 1)
        sums = [
            (near[cut].astype(jnp.float32) + far_in[cut].astype(jnp.float32)).astype(jnp.bfloat16)
            for cut in cuts
        ]
        crossed = []
        for c in range(CHUNKS):
            crossed.append(swapped(sums[c], "head", 2))
        advanced_parts = []
        sent = []
        for c, part in enumerate(hidden):
            latent = latents[k] if k < last else None
            onward, *advanced = update(
                k, cuts[c].start, steps, own, side_in, crossed[c], part, latent, mods
            )
            advanced_parts += advanced
            sent.append(shifted(onward, "segment", 1))
        hidden = sent
        if k == 0:
            kept = advanced_parts
        elif k < last:
            done = jnp.concatenate(advanced_parts, axis=0)
    return finish(cuts, steps, latent_in, hidden, kept, moved)


def normalize(hidden_rows, shift_vec, scale_vec):
    values_f32 = hidden_rows.astype(jnp.float32)
    center = jnp.mean(values_f32, axis=-1, keepdims=True)
    centered = values_f32 - center
    variance = jnp.mean(centered * centered, axis=-1, keepdims=True)
    return (centered * lax.rsqrt(variance + 1e-06) * (1.0 + scale_vec) + shift_vec).astype(
        jnp.bfloat16
    )


def pick_value(table_row, index_value):
    positions = jnp.arange(table_row.shape[0], dtype=jnp.int32)
    return jnp.sum(jnp.where(positions == index_value, table_row, jnp.zeros_like(table_row)))


def local_general(
    hidden_in,
    latent_in,
    key_values,
    qkv_weight,
    out_weight,
    modulation,
    step_sizes,
    patch_order,
    tick_patch,
    step_ids,
):
    segment_index = lax.axis_index("segment")
    last_segment = lax.axis_size("segment") - 1
    local_width = out_weight.shape[1]
    model_width = out_weight.shape[2]
    column = lax.axis_index("head") * local_width
    heads_here = local_width // HEAD_DIM
    patch_rows = hidden_in.shape[0]
    weights_local = qkv_weight[0].reshape(model_width, 3 * local_width)
    projection = out_weight[0]
    step_table = modulation[0]
    layer_cache = key_values[0]
    tokens = layer_cache.shape[1]
    is_last = segment_index == last_segment
    part_hidden, part_latent = (hidden_in, latent_in)
    for tick_number in range(tick_patch.shape[0]):
        position = pick_value(tick_patch[tick_number], segment_index)
        patch_index = pick_value(patch_order, position)
        step_index = pick_value(step_ids[tick_number], segment_index)
        mods = lax.dynamic_index_in_dim(step_table, step_index, 0, keepdims=False)
        step_size = pick_value(step_sizes, step_index)
        patch_index, mods, step_size = (patch_index, mods, step_size)
        full_hidden = lax.all_gather(part_hidden, "head", axis=1, tiled=True)
        current_cache = layer_cache
        normed = normalize(full_hidden, mods[0], mods[1])
        projected = jnp.dot(normed, weights_local, preferred_element_type=jnp.float32)
        projected = projected.astype(jnp.bfloat16).reshape(patch_rows, 3, local_width)
        fresh_rows = jnp.stack([projected[:, 1], projected[:, 2]])
        zero_index = jnp.zeros((), jnp.int32)
        current_cache = lax.dynamic_update_slice(
            current_cache, fresh_rows, (zero_index, patch_index * patch_rows, zero_index)
        )
        queries = projected[:, 0].reshape(patch_rows, heads_here, HEAD_DIM)
        cached_keys = current_cache[0].reshape(tokens, heads_here, HEAD_DIM)
        cached_values = current_cache[1].reshape(tokens, heads_here, HEAD_DIM)
        scores = jnp.einsum(
            "phd,lhd->hpl", queries, cached_keys, preferred_element_type=jnp.float32
        ) * HEAD_DIM ** (-0.5)
        highest = jnp.max(scores, axis=-1, keepdims=True)
        expo = jnp.exp(scores - highest)
        attention = (expo / jnp.sum(expo, axis=-1, keepdims=True)).astype(jnp.bfloat16)
        head_out = jnp.einsum(
            "hpl,lhd->phd", attention, cached_values, preferred_element_type=jnp.float32
        )
        head_out = head_out.astype(jnp.bfloat16).reshape(patch_rows, local_width)
        partial_value = jnp.dot(head_out, projection, preferred_element_type=jnp.float32)
        partial_value, layer_cache = (partial_value, current_cache)
        attended = lax.psum_scatter(
            partial_value.astype(jnp.bfloat16), "head", scatter_dimension=1, tiled=True
        ).astype(jnp.float32)
        gate_cols = lax.dynamic_slice_in_dim(mods[2], column, local_width, 0)
        updated = (part_hidden.astype(jnp.float32) + (1.0 + gate_cols) * attended).astype(
            jnp.bfloat16
        )
        advanced = (
            part_latent.astype(jnp.float32) + step_size * updated.astype(jnp.float32)
        ).astype(jnp.bfloat16)
        send_hidden = jnp.where(is_last, advanced, updated)
        send_latent = jnp.where(is_last, advanced, part_latent)
        part_hidden, part_latent = shifted((send_hidden, send_latent), "segment", 1)
    return (part_hidden, part_latent)


def solution(mesh):
    shape = mesh.shape

    def local(*args):
        hidden_in, ticks = args[0], args[8].shape[0]
        fits = (
            shape["head"] == 4
            and hidden_in.shape[1] % LANES == 0
            and hidden_in.shape[0] % (16 * CHUNKS) == 0
            and ticks == shape["segment"]
            and ticks > 1
        )
        return local_fast(*args) if fits else local_general(*args)

    return jax.shard_map(
        local,
        mesh=mesh,
        in_specs=(
            P(("groups", "segment"), "head"),
            P(("groups", "segment"), "head"),
            P(("groups", "segment"), None, None, "head"),
            P("segment", None, None, "head"),
            P("segment", "head", None),
            P("segment", None, None, None),
            P(),
            P("groups"),
            P("groups", None),
            P("groups", None),
        ),
        out_specs=(P(("groups", "segment"), "head"), P(("groups", "segment"), "head")),
        check_vma=False,
    )
```

```python
import functools

import jax
import jax.numpy as jnp
from jax import lax
from jax.experimental import pallas as pl
from jax.experimental.pallas import tpu as pltpu
from jax.sharding import PartitionSpec as P


HEAD_DIM = 64
LANES = 128
CHUNKS = 2
VMEM_BYTES = 12 << 20

IN_VMEM = pl.BlockSpec(memory_space=pltpu.VMEM)
ANYWHERE = pl.BlockSpec(memory_space=pl.ANY)


def shifted(value, axis, steps):
    count = lax.axis_size(axis)
    pairs = [(source, (source + steps) % count) for source in range(count)]
    return lax.ppermute(value, axis, pairs)


def swapped(value, axis, bit):
    return lax.ppermute(value, axis, [(i, i ^ bit) for i in range(lax.axis_size(axis))])


def position(axis):
    return lax.axis_index(axis).astype(jnp.int32)


def entry(row, index):
    row = row.astype(jnp.float32)
    hit = lax.broadcasted_iota(jnp.int32, row.shape, 1) == index
    return jnp.sum(jnp.where(hit, row, jnp.zeros_like(row)))


def whole(row, index):
    return entry(row, index).astype(jnp.int32)


def preload_kernel(weight, kept, sem):
    copy = pltpu.make_async_copy(weight, kept, sem)
    copy.start()
    copy.wait()


def preload(weight):
    return pl.pallas_call(
        preload_kernel,
        out_shape=pltpu.VMEM(weight.shape, weight.dtype),
        in_specs=[pl.BlockSpec(memory_space=pltpu.HBM)],
        out_specs=IN_VMEM,
        scratch_shapes=[pltpu.SemaphoreType.DMA],
        compiler_params=pltpu.CompilerParams(vmem_limit_bytes=VMEM_BYTES),
        cost_estimate=pl.CostEstimate(flops=0, bytes_accessed=4 * weight.size, transcendentals=0),
        name="preload",
    )(weight)


def project_kernel(width, tick, step_ids, x0, x1, x2, x3, mods, weight, queries, fresh, normed):
    me, segment = position("head"), position("segment")
    step = whole(step_ids[tick : tick + 1, :], segment)
    shares = (x0, x1, x2, x3)
    rows = x0.shape[0]
    features = len(shares) * width
    total = jnp.zeros((rows, 1), jnp.float32)
    for share in shares:
        total += jnp.sum(share[...].astype(jnp.float32), axis=-1, keepdims=True)
    center = total / features
    squares = jnp.zeros((rows, 1), jnp.float32)
    for share in shares:
        centered = share[...].astype(jnp.float32) - center
        squares += jnp.sum(centered * centered, axis=-1, keepdims=True)
    inverse = lax.rsqrt(squares / features + 1e-06)
    for j, share in enumerate(shares):
        at = pl.multiple_of((me ^ j) * width, width)
        centered = share[...].astype(jnp.float32) - center
        shift = mods[0, pl.ds(step, 1), pl.ds(at, width)]
        scale = mods[1, pl.ds(step, 1), pl.ds(at, width)]
        normed[:, pl.ds(at, width)] = (centered * inverse * (1.0 + scale) + shift).astype(
            jnp.bfloat16
        )
    queries[...] = jnp.dot(
        normed[...], weight[0], preferred_element_type=jnp.float32
    ).astype(jnp.bfloat16)

    @pl.loop(0, fresh.shape[0])
    def _(i):
        fresh[i] = jnp.dot(
            normed[...], weight[i + 1], preferred_element_type=jnp.float32
        ).astype(jnp.bfloat16)


def project(tick, step_ids, shares, mods, weight):
    rows, width = shares[0].shape
    return pl.pallas_call(
        functools.partial(project_kernel, width, tick),
        out_shape=(
            jax.ShapeDtypeStruct((rows, width), jnp.bfloat16),
            jax.ShapeDtypeStruct((2, rows, width), jnp.bfloat16),
        ),
        in_specs=[IN_VMEM] * 7,
        out_specs=(IN_VMEM,) * 2,
        scratch_shapes=[pltpu.VMEM((rows, 4 * width), jnp.bfloat16)],
        compiler_params=pltpu.CompilerParams(vmem_limit_bytes=VMEM_BYTES),
        cost_estimate=pl.CostEstimate(
            flops=2 * rows * 12 * width * width, bytes_accessed=14 * rows * width, transcendentals=0
        ),
        name="project",
    )(step_ids, *shares, mods, weight)


def attend_kernel(tick, chunks, extra, *refs):
    tick_patch, patch_order, old, weight = refs[:4]
    queries, fresh = refs[4 : 4 + 2 * chunks : 2], refs[5 : 4 + 2 * chunks : 2]
    far, heads, cache, even, odd = refs[4 + 2 * chunks + extra :]
    me, segment = position("head"), position("segment")
    patch = whole(patch_order[...], whole(tick_patch[tick : tick + 1, :], segment))
    rows, width = heads.shape

    @pl.loop(0, cache.shape[1] // rows)
    def _(block):
        cut = pl.ds(pl.multiple_of(block * rows, rows), rows)
        cache[:, cut, :] = old[:, cut, :]

    start = 0
    for part in fresh:
        at = pl.multiple_of(patch * rows + start, 16)
        cache[:, pl.ds(at, part.shape[1]), :] = part[...]
        start += part.shape[1]
    low = lax.broadcasted_iota(jnp.int32, (rows, LANES), 1) < HEAD_DIM
    zero = jnp.zeros((rows, LANES), jnp.bfloat16)
    ones = jnp.ones((cache.shape[1], LANES), jnp.bfloat16)

    def columns(pair):
        return pl.ds(pl.multiple_of(pair * LANES, LANES), LANES)

    def score(pair, scores):
        cols = columns(pair)
        query = jnp.concatenate([q[:, cols] for q in queries], axis=0) * jnp.bfloat16(
            HEAD_DIM**-0.5
        )
        both = jnp.concatenate(
            [jnp.where(low, query, zero), jnp.where(low, zero, query)], axis=0
        )
        scores[...] = lax.dot_general(
            both,
            cache[0, :, cols],
            (((1,), (1,)), ((), ())),
            preferred_element_type=jnp.float32,
        )

    def mix(pair, scores):
        cols = columns(pair)
        highest = jnp.max(scores[...], axis=-1, keepdims=True)
        expo = jnp.exp(scores[...] - highest).astype(jnp.bfloat16)
        mixed = jnp.dot(
            expo,
            jnp.concatenate([cache[1, :, cols], ones], axis=1),
            preferred_element_type=jnp.float32,
        )
        out = mixed[:, :LANES] / mixed[:, LANES:]
        heads[:, cols] = jnp.where(low, out[:rows], out[rows:]).astype(jnp.bfloat16)

    pairs = width // LANES
    score(0, even)

    @pl.loop(0, pairs // 2)
    def _(i):
        score(2 * i + 1, odd)
        mix(2 * i, even)
        score(jnp.minimum(2 * i + 2, pairs - 1), even)
        mix(2 * i + 1, odd)

    if pairs % 2:
        mix(pairs - 1, even)
    at = pl.multiple_of((me ^ 3) * width, width)
    far[...] = jnp.dot(
        heads[...], weight[:, pl.ds(at, width)], preferred_element_type=jnp.float32
    ).astype(jnp.bfloat16)


def attend(tick, plan, fresh, cache, weight, arrived, final):
    rows = sum(queries.shape[0] for queries, _ in fresh)
    _, tokens, width = cache.shape
    out = jax.ShapeDtypeStruct((rows, width), jnp.bfloat16)
    kept = jax.ShapeDtypeStruct(cache.shape, cache.dtype)
    return pl.pallas_call(
        functools.partial(attend_kernel, tick, len(fresh), len(arrived)),
        out_shape=(out, out) + (() if final else (kept,)),
        in_specs=[IN_VMEM] * (4 + 2 * len(fresh)) + [ANYWHERE] * len(arrived),
        out_specs=(IN_VMEM,) * (2 if final else 3),
        scratch_shapes=([pltpu.VMEM(cache.shape, cache.dtype)] if final else [])
        + [pltpu.VMEM((2 * rows, tokens), jnp.float32)] * 2,
        compiler_params=pltpu.CompilerParams(vmem_limit_bytes=VMEM_BYTES),
        cost_estimate=pl.CostEstimate(
            flops=2 * rows * width * (8 * tokens + 2 * width),
            bytes_accessed=14 * rows * width,
            transcendentals=rows * tokens * width // HEAD_DIM,
        ),
        name="attend",
    )(*plan, cache, weight, *[array for part in fresh for array in part], *arrived)


def output_kernel(heads, weight, out):
    me = position("head")
    width = heads.shape[1]

    @pl.loop(0, out.shape[0])
    def _(j):
        at = pl.multiple_of((me ^ j) * width, width)
        out[j] = jnp.dot(
            heads[...], weight[:, pl.ds(at, width)], preferred_element_type=jnp.float32
        ).astype(jnp.bfloat16)


def output(heads, weight):
    return pl.pallas_call(
        output_kernel,
        out_shape=jax.ShapeDtypeStruct((3,) + heads.shape, heads.dtype),
        in_specs=[IN_VMEM] * 2,
        out_specs=IN_VMEM,
        compiler_params=pltpu.CompilerParams(vmem_limit_bytes=VMEM_BYTES),
        cost_estimate=pl.CostEstimate(
            flops=6 * heads.size * heads.shape[1], bytes_accessed=6 * heads.size, transcendentals=0
        ),
        name="output",
    )(heads, weight)


def update_kernel(
    tick, start, step_ids, step_sizes, own, side, arrived, hidden, latent, mods, sent, advanced
):
    me, segment = position("head"), position("segment")
    rows, width = hidden.shape
    step = whole(step_ids[tick : tick + 1, :], segment)
    cut = pl.ds(start, rows)
    attended = (
        own[cut, :].astype(jnp.float32)
        + side[cut, :].astype(jnp.float32)
        + arrived[...].astype(jnp.float32)
    )
    at = pl.multiple_of(me * width, width)
    gate = 1.0 + mods[2, pl.ds(step, 1), pl.ds(at, width)]
    updated = (hidden[...].astype(jnp.float32) + gate * attended).astype(jnp.bfloat16)
    sent[...] = updated
    if advanced is not None:
        moved = (
            latent[cut, :].astype(jnp.float32) + entry(step_sizes[...], step) * updated.astype(jnp.float32)
        ).astype(jnp.bfloat16)
        advanced[...] = moved
        is_last = segment == lax.axis_size("segment") - 1

        @pl.when(is_last)
        def _():
            sent[...] = moved


def update(tick, start, tables, own, side, arrived, hidden, latent, mods):
    out = jax.ShapeDtypeStruct(hidden.shape, hidden.dtype)
    if latent is None:

        def body(*refs):
            update_kernel(tick, start, *refs[:6], None, *refs[6:8], None)

        arrays, outs = (own, side, arrived, hidden, mods), 1
    else:
        body = functools.partial(update_kernel, tick, start)
        arrays, outs = (own, side, arrived, hidden, latent, mods), 2
    return pl.pallas_call(
        body,
        out_shape=(out,) * outs,
        in_specs=[IN_VMEM] * (2 + len(arrays)),
        out_specs=(IN_VMEM,) * outs,
        compiler_params=pltpu.CompilerParams(vmem_limit_bytes=VMEM_BYTES),
        cost_estimate=pl.CostEstimate(
            flops=8 * hidden.size, bytes_accessed=16 * hidden.size, transcendentals=0
        ),
        name="update",
    )(*tables, *arrays)


def finish_kernel(cuts, count, step_ids, step_sizes, latent, *refs):
    segment = position("segment")
    last = lax.axis_size("segment") - 1
    parts = refs[: len(cuts)]
    kept = refs[len(cuts) : 2 * len(cuts)]
    moved = refs[2 * len(cuts) : 2 * len(cuts) + count]
    out_hidden, out_latent = refs[2 * len(cuts) + count :]
    for cut, part, piece in zip(cuts, parts, kept):
        out_hidden[cut, :] = part[...]
        out_latent[cut, :] = piece[...]
    for k, array in enumerate(moved):

        @pl.when(segment == last - 1 - k)
        def _():
            out_latent[...] = array[...]

    @pl.when(segment == 0)
    def _():
        step_size = entry(step_sizes[...], whole(step_ids[step_ids.shape[0] - 1 :, :], last))
        for cut, part in zip(cuts, parts):
            advanced = (
                latent[cut, :].astype(jnp.float32) + step_size * part[...].astype(jnp.float32)
            ).astype(jnp.bfloat16)
            out_hidden[cut, :] = advanced
            out_latent[cut, :] = advanced


def finish(cuts, tables, latent, parts, kept, moved):
    out = jax.ShapeDtypeStruct(latent.shape, latent.dtype)
    arrays = (latent, *parts, *kept, *moved)
    return pl.pallas_call(
        functools.partial(finish_kernel, cuts, len(moved)),
        out_shape=(out, out),
        in_specs=[IN_VMEM] * (2 + len(arrays)),
        out_specs=(IN_VMEM, IN_VMEM),
        compiler_params=pltpu.CompilerParams(vmem_limit_bytes=VMEM_BYTES),
        name="finish",
    )(*tables, *arrays)


def local_fast(
    hidden_in,
    latent_in,
    key_values,
    qkv_weight,
    out_weight,
    modulation,
    step_sizes,
    patch_order,
    tick_patch,
    step_ids,
):
    last = lax.axis_size("segment") - 1
    ticks = tick_patch.shape[0]
    rows = hidden_in.shape[0]
    weight = jnp.transpose(qkv_weight[0], (1, 0, 2))
    mods = jnp.transpose(modulation[0], (1, 0, 2))
    projection = out_weight[0]
    weight = preload(weight)
    cache = key_values[0]
    plan = (tick_patch, patch_order.reshape(1, -1))
    steps = (step_ids, step_sizes.reshape(1, -1))

    step_rows = rows // CHUNKS
    cuts = [slice(c * step_rows, (c + 1) * step_rows) for c in range(CHUNKS)]
    hidden = [hidden_in[cut] for cut in cuts]
    latents = {0: latent_in}
    kept, moved = [], []
    done = None
    for k in range(ticks):
        if done is not None:
            moved.append(lax.ppermute(done, "segment", [(last, last + 1 - k)]))
            done = None
        if k + 1 < last:
            latents[k + 1] = lax.ppermute(latent_in, "segment", [(last - k - 1, last)])
        fresh = []
        for part in hidden:
            across = swapped(part, "head", 2)
            beside = swapped(part, "head", 1)
            if fresh:
                across, _ = lax.optimization_barrier((across, fresh[-1][0]))
            corner = swapped(across, "head", 1)
            fresh.append(
                project(k, step_ids, (part, beside, across, corner), mods, weight)
            )
        arrived = moved[:-1]
        far, heads, *rest = attend(k, plan, fresh, cache, projection, arrived, k == ticks - 1)
        if rest:
            cache = rest[0]
        far_in = swapped(far, "head", 1)
        own, side, near = output(heads, projection)
        side_in = swapped(side, "head", 1)
        sums = [
            (near[cut].astype(jnp.float32) + far_in[cut].astype(jnp.float32)).astype(jnp.bfloat16)
            for cut in cuts
        ]
        crossed = []
        for c in range(CHUNKS):
            crossed.append(swapped(sums[c], "head", 2))
        advanced_parts = []
        sent = []
        for c, part in enumerate(hidden):
            latent = latents[k] if k < last else None
            onward, *advanced = update(
                k, cuts[c].start, steps, own, side_in, crossed[c], part, latent, mods
            )
            advanced_parts += advanced
            sent.append(shifted(onward, "segment", 1))
        hidden = sent
        if k == 0:
            kept = advanced_parts
        elif k < last:
            done = jnp.concatenate(advanced_parts, axis=0)
    return finish(cuts, steps, latent_in, hidden, kept, moved)


def normalize(hidden_rows, shift_vec, scale_vec):
    values_f32 = hidden_rows.astype(jnp.float32)
    center = jnp.mean(values_f32, axis=-1, keepdims=True)
    centered = values_f32 - center
    variance = jnp.mean(centered * centered, axis=-1, keepdims=True)
    return (centered * lax.rsqrt(variance + 1e-06) * (1.0 + scale_vec) + shift_vec).astype(
        jnp.bfloat16
    )


def pick_value(table_row, index_value):
    positions = jnp.arange(table_row.shape[0], dtype=jnp.int32)
    return jnp.sum(jnp.where(positions == index_value, table_row, jnp.zeros_like(table_row)))


def local_general(
    hidden_in,
    latent_in,
    key_values,
    qkv_weight,
    out_weight,
    modulation,
    step_sizes,
    patch_order,
    tick_patch,
    step_ids,
):
    segment_index = lax.axis_index("segment")
    last_segment = lax.axis_size("segment") - 1
    local_width = out_weight.shape[1]
    model_width = out_weight.shape[2]
    column = lax.axis_index("head") * local_width
    heads_here = local_width // HEAD_DIM
    patch_rows = hidden_in.shape[0]
    weights_local = qkv_weight[0].reshape(model_width, 3 * local_width)
    projection = out_weight[0]
    step_table = modulation[0]
    layer_cache = key_values[0]
    tokens = layer_cache.shape[1]
    is_last = segment_index == last_segment
    part_hidden, part_latent = (hidden_in, latent_in)
    for tick_number in range(tick_patch.shape[0]):
        position = pick_value(tick_patch[tick_number], segment_index)
        patch_index = pick_value(patch_order, position)
        step_index = pick_value(step_ids[tick_number], segment_index)
        mods = lax.dynamic_index_in_dim(step_table, step_index, 0, keepdims=False)
        step_size = pick_value(step_sizes, step_index)
        patch_index, mods, step_size = (patch_index, mods, step_size)
        full_hidden = lax.all_gather(part_hidden, "head", axis=1, tiled=True)
        current_cache = layer_cache
        normed = normalize(full_hidden, mods[0], mods[1])
        projected = jnp.dot(normed, weights_local, preferred_element_type=jnp.float32)
        projected = projected.astype(jnp.bfloat16).reshape(patch_rows, 3, local_width)
        fresh_rows = jnp.stack([projected[:, 1], projected[:, 2]])
        zero_index = jnp.zeros((), jnp.int32)
        current_cache = lax.dynamic_update_slice(
            current_cache, fresh_rows, (zero_index, patch_index * patch_rows, zero_index)
        )
        queries = projected[:, 0].reshape(patch_rows, heads_here, HEAD_DIM)
        cached_keys = current_cache[0].reshape(tokens, heads_here, HEAD_DIM)
        cached_values = current_cache[1].reshape(tokens, heads_here, HEAD_DIM)
        scores = jnp.einsum(
            "phd,lhd->hpl", queries, cached_keys, preferred_element_type=jnp.float32
        ) * HEAD_DIM ** (-0.5)
        highest = jnp.max(scores, axis=-1, keepdims=True)
        expo = jnp.exp(scores - highest)
        attention = (expo / jnp.sum(expo, axis=-1, keepdims=True)).astype(jnp.bfloat16)
        head_out = jnp.einsum(
            "hpl,lhd->phd", attention, cached_values, preferred_element_type=jnp.float32
        )
        head_out = head_out.astype(jnp.bfloat16).reshape(patch_rows, local_width)
        partial_value = jnp.dot(head_out, projection, preferred_element_type=jnp.float32)
        partial_value, layer_cache = (partial_value, current_cache)
        attended = lax.psum_scatter(
            partial_value.astype(jnp.bfloat16), "head", scatter_dimension=1, tiled=True
        ).astype(jnp.float32)
        gate_cols = lax.dynamic_slice_in_dim(mods[2], column, local_width, 0)
        updated = (part_hidden.astype(jnp.float32) + (1.0 + gate_cols) * attended).astype(
            jnp.bfloat16
        )
        advanced = (
            part_latent.astype(jnp.float32) + step_size * updated.astype(jnp.float32)
        ).astype(jnp.bfloat16)
        send_hidden = jnp.where(is_last, advanced, updated)
        send_latent = jnp.where(is_last, advanced, part_latent)
        part_hidden, part_latent = shifted((send_hidden, send_latent), "segment", 1)
    return (part_hidden, part_latent)


def solution(mesh):
    shape = mesh.shape

    def local(*args):
        hidden_in, ticks = args[0], args[8].shape[0]
        fits = (
            shape["head"] == 4
            and hidden_in.shape[1] % LANES == 0
            and hidden_in.shape[0] % (16 * CHUNKS) == 0
            and ticks == shape["segment"]
            and ticks > 1
        )
        return local_fast(*args) if fits else local_general(*args)

    return jax.shard_map(
        local,
        mesh=mesh,
        in_specs=(
            P(("groups", "segment"), "head"),
            P(("groups", "segment"), "head"),
            P(("groups", "segment"), None, None, "head"),
            P("segment", None, None, "head"),
            P("segment", "head", None),
            P("segment", None, None, None),
            P(),
            P("groups"),
            P("groups", None),
            P("groups", None),
        ),
        out_specs=(P(("groups", "segment"), "head"), P(("groups", "segment"), "head")),
        check_vma=False,
    )
```

```python
import functools

import jax
import jax.numpy as jnp
from jax import lax
from jax.experimental import pallas as pl
from jax.experimental.pallas import tpu as pltpu
from jax.sharding import PartitionSpec as P


HEAD_DIM = 64
LANES = 128
CHUNKS = 2
LAST_CHUNKS = 4
VMEM_BYTES = 12 << 20

IN_VMEM = pl.BlockSpec(memory_space=pltpu.VMEM)
ANYWHERE = pl.BlockSpec(memory_space=pl.ANY)


def shifted(value, axis, steps):
    count = lax.axis_size(axis)
    pairs = [(source, (source + steps) % count) for source in range(count)]
    return lax.ppermute(value, axis, pairs)


def swapped(value, axis, bit):
    return lax.ppermute(value, axis, [(i, i ^ bit) for i in range(lax.axis_size(axis))])


def position(axis):
    return lax.axis_index(axis).astype(jnp.int32)


def entry(row, index):
    row = row.astype(jnp.float32)
    hit = lax.broadcasted_iota(jnp.int32, row.shape, 1) == index
    return jnp.sum(jnp.where(hit, row, jnp.zeros_like(row)))


def whole(row, index):
    return entry(row, index).astype(jnp.int32)


def preload_kernel(weight, kept, sem):
    copy = pltpu.make_async_copy(weight, kept, sem)
    copy.start()
    copy.wait()


def preload(weight):
    return pl.pallas_call(
        preload_kernel,
        out_shape=pltpu.VMEM(weight.shape, weight.dtype),
        in_specs=[pl.BlockSpec(memory_space=pltpu.HBM)],
        out_specs=IN_VMEM,
        scratch_shapes=[pltpu.SemaphoreType.DMA],
        compiler_params=pltpu.CompilerParams(vmem_limit_bytes=38 << 20),
        cost_estimate=pl.CostEstimate(flops=0, bytes_accessed=4 * weight.size, transcendentals=0),
        name="preload",
    )(weight)


def project_kernel(width, tick, step_ids, x0, x1, x2, x3, mods, weight, queries, fresh, normed):
    me, segment = position("head"), position("segment")
    step = whole(step_ids[tick : tick + 1, :], segment)
    shares = (x0, x1, x2, x3)
    rows = x0.shape[0]
    features = len(shares) * width
    total = jnp.zeros((rows, 1), jnp.float32)
    for share in shares:
        total += jnp.sum(share[...].astype(jnp.float32), axis=-1, keepdims=True)
    center = total / features
    squares = jnp.zeros((rows, 1), jnp.float32)
    for share in shares:
        centered = share[...].astype(jnp.float32) - center
        squares += jnp.sum(centered * centered, axis=-1, keepdims=True)
    inverse = lax.rsqrt(squares / features + 1e-06)
    for j, share in enumerate(shares):
        at = pl.multiple_of((me ^ j) * width, width)
        centered = share[...].astype(jnp.float32) - center
        shift = mods[0, pl.ds(step, 1), pl.ds(at, width)]
        scale = mods[1, pl.ds(step, 1), pl.ds(at, width)]
        normed[:, pl.ds(at, width)] = (centered * inverse * (1.0 + scale) + shift).astype(
            jnp.bfloat16
        )
    queries[...] = jnp.dot(
        normed[...], weight[0], preferred_element_type=jnp.float32
    ).astype(jnp.bfloat16)

    @pl.loop(0, fresh.shape[0])
    def _(i):
        fresh[i] = jnp.dot(
            normed[...], weight[i + 1], preferred_element_type=jnp.float32
        ).astype(jnp.bfloat16)


def project(tick, step_ids, shares, mods, weight):
    rows, width = shares[0].shape
    return pl.pallas_call(
        functools.partial(project_kernel, width, tick),
        out_shape=(
            jax.ShapeDtypeStruct((rows, width), jnp.bfloat16),
            jax.ShapeDtypeStruct((2, rows, width), jnp.bfloat16),
        ),
        in_specs=[IN_VMEM] * 7,
        out_specs=(IN_VMEM,) * 2,
        scratch_shapes=[pltpu.VMEM((rows, 4 * width), jnp.bfloat16)],
        compiler_params=pltpu.CompilerParams(vmem_limit_bytes=VMEM_BYTES),
        cost_estimate=pl.CostEstimate(
            flops=2 * rows * 12 * width * width, bytes_accessed=14 * rows * width, transcendentals=0
        ),
        name="project",
    )(step_ids, *shares, mods, weight)


def attend_kernel(tick, chunks, extra, *refs):
    tick_patch, patch_order, old, weight = refs[:4]
    queries, fresh = refs[4 : 4 + 2 * chunks : 2], refs[5 : 4 + 2 * chunks : 2]
    far, heads, cache, even, odd = refs[4 + 2 * chunks + extra :]
    me, segment = position("head"), position("segment")
    patch = whole(patch_order[...], whole(tick_patch[tick : tick + 1, :], segment))
    rows, width = heads.shape

    @pl.loop(0, cache.shape[1] // rows)
    def _(block):
        cut = pl.ds(pl.multiple_of(block * rows, rows), rows)
        cache[:, cut, :] = old[:, cut, :]

    start = 0
    for part in fresh:
        at = pl.multiple_of(patch * rows + start, 16)
        cache[:, pl.ds(at, part.shape[1]), :] = part[...]
        start += part.shape[1]
    low = lax.broadcasted_iota(jnp.int32, (rows, LANES), 1) < HEAD_DIM
    zero = jnp.zeros((rows, LANES), jnp.bfloat16)
    ones = jnp.ones((cache.shape[1], LANES), jnp.bfloat16)

    def columns(pair):
        return pl.ds(pl.multiple_of(pair * LANES, LANES), LANES)

    def score(pair, scores):
        cols = columns(pair)
        query = jnp.concatenate([q[:, cols] for q in queries], axis=0) * jnp.bfloat16(
            HEAD_DIM**-0.5
        )
        both = jnp.concatenate(
            [jnp.where(low, query, zero), jnp.where(low, zero, query)], axis=0
        )
        scores[...] = lax.dot_general(
            both,
            cache[0, :, cols],
            (((1,), (1,)), ((), ())),
            preferred_element_type=jnp.float32,
        )

    def mix(pair, scores):
        cols = columns(pair)
        highest = jnp.max(scores[...], axis=-1, keepdims=True)
        expo = jnp.exp(scores[...] - highest).astype(jnp.bfloat16)
        mixed = jnp.dot(
            expo,
            jnp.concatenate([cache[1, :, cols], ones], axis=1),
            preferred_element_type=jnp.float32,
        )
        out = mixed[:, :LANES] / mixed[:, LANES:]
        heads[:, cols] = jnp.where(low, out[:rows], out[rows:]).astype(jnp.bfloat16)

    pairs = width // LANES
    score(0, even)

    @pl.loop(0, pairs // 2)
    def _(i):
        score(2 * i + 1, odd)
        mix(2 * i, even)
        score(jnp.minimum(2 * i + 2, pairs - 1), even)
        mix(2 * i + 1, odd)

    if pairs % 2:
        mix(pairs - 1, even)
    at = pl.multiple_of((me ^ 3) * width, width)
    far[...] = jnp.dot(
        heads[...], weight[:, pl.ds(at, width)], preferred_element_type=jnp.float32
    ).astype(jnp.bfloat16)


def attend(tick, plan, fresh, cache, weight, arrived, final):
    rows = sum(queries.shape[0] for queries, _ in fresh)
    _, tokens, width = cache.shape
    out = jax.ShapeDtypeStruct((rows, width), jnp.bfloat16)
    kept = jax.ShapeDtypeStruct(cache.shape, cache.dtype)
    return pl.pallas_call(
        functools.partial(attend_kernel, tick, len(fresh), len(arrived)),
        out_shape=(out, out) + (() if final else (kept,)),
        in_specs=[IN_VMEM] * (4 + 2 * len(fresh)) + [ANYWHERE] * len(arrived),
        out_specs=(IN_VMEM,) * (2 if final else 3),
        scratch_shapes=([pltpu.VMEM(cache.shape, cache.dtype)] if final else [])
        + [pltpu.VMEM((2 * rows, tokens), jnp.float32)] * 2,
        compiler_params=pltpu.CompilerParams(vmem_limit_bytes=VMEM_BYTES),
        cost_estimate=pl.CostEstimate(
            flops=2 * rows * width * (8 * tokens + 2 * width),
            bytes_accessed=14 * rows * width,
            transcendentals=rows * tokens * width // HEAD_DIM,
        ),
        name="attend",
    )(*plan, cache, weight, *[array for part in fresh for array in part], *arrived)


def output_kernel(heads, weight, out):
    me = position("head")
    width = heads.shape[1]

    @pl.loop(0, out.shape[0])
    def _(j):
        at = pl.multiple_of((me ^ j) * width, width)
        out[j] = jnp.dot(
            heads[...], weight[:, pl.ds(at, width)], preferred_element_type=jnp.float32
        ).astype(jnp.bfloat16)


def output(heads, weight):
    return pl.pallas_call(
        output_kernel,
        out_shape=jax.ShapeDtypeStruct((3,) + heads.shape, heads.dtype),
        in_specs=[IN_VMEM] * 2,
        out_specs=IN_VMEM,
        compiler_params=pltpu.CompilerParams(vmem_limit_bytes=VMEM_BYTES),
        cost_estimate=pl.CostEstimate(
            flops=6 * heads.size * heads.shape[1], bytes_accessed=6 * heads.size, transcendentals=0
        ),
        name="output",
    )(heads, weight)


def update_kernel(
    tick,
    start,
    offset,
    step_ids,
    step_sizes,
    own,
    side,
    arrived,
    hidden,
    latent,
    mods,
    sent,
    advanced,
):
    me, segment = position("head"), position("segment")
    rows, width = arrived.shape
    step = whole(step_ids[tick : tick + 1, :], segment)
    cut = pl.ds(start, rows)
    attended = (
        own[cut, :].astype(jnp.float32)
        + side[cut, :].astype(jnp.float32)
        + arrived[...].astype(jnp.float32)
    )
    at = pl.multiple_of(me * width, width)
    gate = 1.0 + mods[2, pl.ds(step, 1), pl.ds(at, width)]
    before = hidden[pl.ds(offset, rows), :].astype(jnp.float32)
    updated = (before + gate * attended).astype(jnp.bfloat16)
    sent[...] = updated
    if advanced is not None:
        is_last = segment == lax.axis_size("segment") - 1

        @pl.when(is_last)
        def _():
            moved = (
                latent[cut, :].astype(jnp.float32) + entry(step_sizes[...], step) * updated.astype(jnp.float32)
            ).astype(jnp.bfloat16)
            advanced[...] = moved
            sent[...] = moved


def update(tick, start, offset, tables, own, side, arrived, hidden, latent, mods):
    out = jax.ShapeDtypeStruct(arrived.shape, arrived.dtype)
    if latent is None:

        def body(*refs):
            update_kernel(tick, start, offset, *refs[:6], None, *refs[6:8], None)

        arrays, outs = (own, side, arrived, hidden, mods), 1
    else:
        body = functools.partial(update_kernel, tick, start, offset)
        arrays, outs = (own, side, arrived, hidden, latent, mods), 2
    return pl.pallas_call(
        body,
        out_shape=(out,) * outs,
        in_specs=[IN_VMEM] * (2 + len(arrays)),
        out_specs=(IN_VMEM,) * outs,
        compiler_params=pltpu.CompilerParams(vmem_limit_bytes=VMEM_BYTES),
        cost_estimate=pl.CostEstimate(
            flops=8 * arrived.size, bytes_accessed=16 * arrived.size, transcendentals=0
        ),
        name="update",
    )(*tables, *arrays)


def finish_kernel(cuts, kept_cuts, count, step_ids, step_sizes, latent, *refs):
    segment = position("segment")
    last = lax.axis_size("segment") - 1
    parts = refs[: len(cuts)]
    both = len(cuts) + len(kept_cuts)
    kept = refs[len(cuts) : both]
    moved = refs[both : both + count]
    out_hidden, out_latent = refs[both + count :]
    for cut, part in zip(cuts, parts):
        out_hidden[cut, :] = part[...]
    for cut, piece in zip(kept_cuts, kept):
        out_latent[cut, :] = piece[...]
    for k, array in enumerate(moved):

        @pl.when(segment == last - 1 - k)
        def _():
            out_latent[...] = array[...]

    @pl.when(segment == 0)
    def _():
        step_size = entry(step_sizes[...], whole(step_ids[step_ids.shape[0] - 1 :, :], last))
        for cut, part in zip(cuts, parts):
            advanced = (
                latent[cut, :].astype(jnp.float32) + step_size * part[...].astype(jnp.float32)
            ).astype(jnp.bfloat16)
            out_hidden[cut, :] = advanced
            out_latent[cut, :] = advanced


def finish(cuts, kept_cuts, tables, latent, parts, kept, moved):
    out = jax.ShapeDtypeStruct(latent.shape, latent.dtype)
    arrays = (latent, *parts, *kept, *moved)
    return pl.pallas_call(
        functools.partial(finish_kernel, cuts, kept_cuts, len(moved)),
        out_shape=(out, out),
        in_specs=[IN_VMEM] * (2 + len(arrays)),
        out_specs=(IN_VMEM, IN_VMEM),
        compiler_params=pltpu.CompilerParams(vmem_limit_bytes=VMEM_BYTES),
        name="finish",
    )(*tables, *arrays)


def local_fast(
    hidden_in,
    latent_in,
    key_values,
    qkv_weight,
    out_weight,
    modulation,
    step_sizes,
    patch_order,
    tick_patch,
    step_ids,
):
    last = lax.axis_size("segment") - 1
    ticks = tick_patch.shape[0]
    rows = hidden_in.shape[0]
    weight = jnp.transpose(qkv_weight[0], (1, 0, 2))
    mods = jnp.transpose(modulation[0], (1, 0, 2))
    projection = out_weight[0]
    weight = preload(weight)
    cache = key_values[0]
    plan = (tick_patch, patch_order.reshape(1, -1))
    steps = (step_ids, step_sizes.reshape(1, -1))

    step_rows = rows // CHUNKS
    cuts = [slice(c * step_rows, (c + 1) * step_rows) for c in range(CHUNKS)]
    hidden = [hidden_in[cut] for cut in cuts]
    latents = {0: latent_in}
    kept, moved = [], []
    done = None
    for k in range(ticks):
        if done is not None:
            moved.append(lax.ppermute(done, "segment", [(last, last + 1 - k)]))
            done = None
        if k + 1 < last:
            latents[k + 1] = lax.ppermute(latent_in, "segment", [(last - k - 1, last)])
        fresh = []
        for part in hidden:
            across = swapped(part, "head", 2)
            beside = swapped(part, "head", 1)
            if fresh:
                across, _ = lax.optimization_barrier((across, fresh[-1][0]))
            corner = swapped(across, "head", 1)
            fresh.append(
                project(k, step_ids, (part, beside, across, corner), mods, weight)
            )
        arrived = moved[:-1]
        far, heads, *rest = attend(k, plan, fresh, cache, projection, arrived, k == ticks - 1)
        if rest:
            cache = rest[0]
        far_in = swapped(far, "head", 1)
        own, side, near = output(heads, projection)
        side_in = swapped(side, "head", 1)
        count = CHUNKS if k < ticks - 1 else LAST_CHUNKS
        pieces = [slice(c * rows // count, (c + 1) * rows // count) for c in range(count)]
        sums = [
            (near[cut].astype(jnp.float32) + far_in[cut].astype(jnp.float32)).astype(jnp.bfloat16)
            for cut in pieces
        ]
        crossed = []
        for c in range(count):
            crossed.append(swapped(sums[c], "head", 2))
        advanced_parts = []
        sent = []
        for c, cut in enumerate(pieces):
            latent = latents[k] if k < last else None
            part, offset = hidden[cut.start // step_rows], cut.start % step_rows
            onward, *advanced = update(
                k, cut.start, offset, steps, own, side_in, crossed[c], part, latent, mods
            )
            advanced_parts += advanced
            sent.append(shifted(onward, "segment", 1))
        hidden = sent
        if k == 0:
            kept = advanced_parts
        elif k < last:
            done = jnp.concatenate(advanced_parts, axis=0)
    return finish(pieces, cuts, steps, latent_in, hidden, kept, moved)


def normalize(hidden_rows, shift_vec, scale_vec):
    values_f32 = hidden_rows.astype(jnp.float32)
    center = jnp.mean(values_f32, axis=-1, keepdims=True)
    centered = values_f32 - center
    variance = jnp.mean(centered * centered, axis=-1, keepdims=True)
    return (centered * lax.rsqrt(variance + 1e-06) * (1.0 + scale_vec) + shift_vec).astype(
        jnp.bfloat16
    )


def pick_value(table_row, index_value):
    positions = jnp.arange(table_row.shape[0], dtype=jnp.int32)
    return jnp.sum(jnp.where(positions == index_value, table_row, jnp.zeros_like(table_row)))


def local_general(
    hidden_in,
    latent_in,
    key_values,
    qkv_weight,
    out_weight,
    modulation,
    step_sizes,
    patch_order,
    tick_patch,
    step_ids,
):
    segment_index = lax.axis_index("segment")
    last_segment = lax.axis_size("segment") - 1
    local_width = out_weight.shape[1]
    model_width = out_weight.shape[2]
    column = lax.axis_index("head") * local_width
    heads_here = local_width // HEAD_DIM
    patch_rows = hidden_in.shape[0]
    weights_local = qkv_weight[0].reshape(model_width, 3 * local_width)
    projection = out_weight[0]
    step_table = modulation[0]
    layer_cache = key_values[0]
    tokens = layer_cache.shape[1]
    is_last = segment_index == last_segment
    part_hidden, part_latent = (hidden_in, latent_in)
    for tick_number in range(tick_patch.shape[0]):
        position = pick_value(tick_patch[tick_number], segment_index)
        patch_index = pick_value(patch_order, position)
        step_index = pick_value(step_ids[tick_number], segment_index)
        mods = lax.dynamic_index_in_dim(step_table, step_index, 0, keepdims=False)
        step_size = pick_value(step_sizes, step_index)
        patch_index, mods, step_size = (patch_index, mods, step_size)
        full_hidden = lax.all_gather(part_hidden, "head", axis=1, tiled=True)
        current_cache = layer_cache
        normed = normalize(full_hidden, mods[0], mods[1])
        projected = jnp.dot(normed, weights_local, preferred_element_type=jnp.float32)
        projected = projected.astype(jnp.bfloat16).reshape(patch_rows, 3, local_width)
        fresh_rows = jnp.stack([projected[:, 1], projected[:, 2]])
        zero_index = jnp.zeros((), jnp.int32)
        current_cache = lax.dynamic_update_slice(
            current_cache, fresh_rows, (zero_index, patch_index * patch_rows, zero_index)
        )
        queries = projected[:, 0].reshape(patch_rows, heads_here, HEAD_DIM)
        cached_keys = current_cache[0].reshape(tokens, heads_here, HEAD_DIM)
        cached_values = current_cache[1].reshape(tokens, heads_here, HEAD_DIM)
        scores = jnp.einsum(
            "phd,lhd->hpl", queries, cached_keys, preferred_element_type=jnp.float32
        ) * HEAD_DIM ** (-0.5)
        highest = jnp.max(scores, axis=-1, keepdims=True)
        expo = jnp.exp(scores - highest)
        attention = (expo / jnp.sum(expo, axis=-1, keepdims=True)).astype(jnp.bfloat16)
        head_out = jnp.einsum(
            "hpl,lhd->phd", attention, cached_values, preferred_element_type=jnp.float32
        )
        head_out = head_out.astype(jnp.bfloat16).reshape(patch_rows, local_width)
        partial_value = jnp.dot(head_out, projection, preferred_element_type=jnp.float32)
        partial_value, layer_cache = (partial_value, current_cache)
        attended = lax.psum_scatter(
            partial_value.astype(jnp.bfloat16), "head", scatter_dimension=1, tiled=True
        ).astype(jnp.float32)
        gate_cols = lax.dynamic_slice_in_dim(mods[2], column, local_width, 0)
        updated = (part_hidden.astype(jnp.float32) + (1.0 + gate_cols) * attended).astype(
            jnp.bfloat16
        )
        advanced = (
            part_latent.astype(jnp.float32) + step_size * updated.astype(jnp.float32)
        ).astype(jnp.bfloat16)
        send_hidden = jnp.where(is_last, advanced, updated)
        send_latent = jnp.where(is_last, advanced, part_latent)
        part_hidden, part_latent = shifted((send_hidden, send_latent), "segment", 1)
    return (part_hidden, part_latent)


def solution(mesh):
    shape = mesh.shape

    def local(*args):
        hidden_in, ticks = args[0], args[8].shape[0]
        fits = (
            shape["head"] == 4
            and hidden_in.shape[1] % LANES == 0
            and hidden_in.shape[0] % (16 * LAST_CHUNKS) == 0
            and ticks == shape["segment"]
            and ticks > 1
        )
        return local_fast(*args) if fits else local_general(*args)

    return jax.shard_map(
        local,
        mesh=mesh,
        in_specs=(
            P(("groups", "segment"), "head"),
            P(("groups", "segment"), "head"),
            P(("groups", "segment"), None, None, "head"),
            P("segment", None, None, "head"),
            P("segment", "head", None),
            P("segment", None, None, None),
            P(),
            P("groups"),
            P("groups", None),
            P("groups", None),
        ),
        out_specs=(P(("groups", "segment"), "head"), P(("groups", "segment"), "head")),
        check_vma=False,
    )
```
